128 devices in a mesh: row: 8 (over x, core), col: 16 (over z, y).
Axes of the slice: x: 4, y: 4, z: 4, core: 2. Of those that a mesh axis runs over, the one named last changes fastest.
Arguments:
- mask: bfloat16 [256, 4096], P('row', 'col'), may hold values from 0 to 1
- target: int32 [256, 4096], P('row', 'col'), may hold values 0 or 1
- kernels: bfloat16 [8, 2, 33, 33], replicated, may hold values from -0.1875 to 0.1875
- weights: float32 [8], replicated, may hold values from 0.2 to 1
- doses: float32 [8], replicated, may hold values from 0.8 to 1.2
- site_pix: int32 [1024, 768], P('row', 'col'), may hold values from 0 to 8191
- send_count: int32 [8, 2048], P('row', 'col'), may hold values from 0 to 48, as said below
- recv_frag: int32 [1024, 768], P('row', 'col'), may hold values from 0 to 2047
- frag_target: float32 [8, 262144], P(None, ('row', 'col')), may hold values from 0 to 6
Outputs:
- gradient: float32 [256, 4096], P('row', 'col')
- frag_error: float32 [8, 262144], P(None, ('row', 'col'))
The draws below stay inside these ranges and needn't reach their ends.
Inputs may be any that keep to these rules, and one draw needn't show every extreme that they name: `send_count`: no device sends more than 48 live slots to one owner; in every draw one owner receives 48 live slots from every device.
All inputs are finite; a program needn't handle non-finite values. No bound on the sum of `target` on one device may be relied on, other than what follows from the above.
Results may differ from the reference program's by a relative error of at most 0.0045.
Values may be sent and summed in bfloat16 or wider, within the bound.
No kernel may reach another device: no remote copies, remote signals or barrier semaphores. Data moves between devices by JAX's collectives and lax.ppermute only.
A program may use at most 64 MiB of HBM per device.

```python
import math
import jax
import jax.numpy as jnp
from jax import lax

TILE_ROWS = 32
TILE_COLS = 256
CAP = 48
FRAGS = 2048
CONDS = 8
KERNELS = 8
KSIZE = 33
HEIGHT = 256
WIDTH = 4096
N_ROW = 8
N_COL = 16
DEVICES = 128


def draw_send_count(key, part):
    first_key, second_key = jax.random.split(jax.random.fold_in(key, 17))
    counts = jax.random.randint(first_key, (N_ROW, N_COL * DEVICES), 0, CAP + 1)
    heavy = jax.random.randint(second_key, (), 0, DEVICES)
    owner_index = jnp.arange(N_COL * DEVICES) % DEVICES
    return jnp.where(owner_index[None, :] == heavy, CAP, counts).astype(jnp.int32)


def set_ends(entries, own_key, least, high):
    longest = entries.shape.index(max(entries.shape))
    spots = []
    for shift in (0, 1):
        where = [jax.random.randint(jax.random.fold_in(own_key, axis), (), 0, length) for axis, length in enumerate(entries.shape)]
        where[longest] = (where[longest] + shift) % entries.shape[longest]
        spots.append(tuple(where))
    return entries.at[spots[0]].set(least).at[spots[1]].set(high)


def shard_levels(stream_key, shape, cuts, least, largest):
    def one(axis_at, shards_of):
        draws = jax.random.uniform(jax.random.fold_in(jax.random.fold_in(stream_key, 6), axis_at), (shards_of,), jnp.float32, least / len(cuts), largest / len(cuts))
        return jnp.repeat(jnp.exp(draws), shape[axis_at] // shards_of).reshape((-1,) + (1,) * (len(shape) - axis_at - 1))

    factor_of = one(*cuts[0])
    for cut in cuts[1:]:
        factor_of = factor_of * one(*cut)
    return factor_of


def noise(stream_key, shape, width, most, held_as=jnp.bfloat16):
    return jnp.clip(width * jax.random.normal(stream_key, shape, jnp.float32), -most, most).astype(held_as)


def setup_inputs(seed: int = 0) -> dict:
    key_of = jax.random.split(jax.random.key(seed), 10)
    return {
        "mask": jnp.clip(1.0 * jax.random.uniform(key_of[0], (HEIGHT, WIDTH), jnp.float32) ** shard_levels(key_of[0], (HEIGHT, WIDTH), ((0, 8), (1, 16)), -0.2, 0.2), 0.0, 1.0).astype(jnp.bfloat16),
        "target": set_ends((jax.random.randint(key_of[1], (HEIGHT, WIDTH), 0, 2) < 1).astype(jnp.int32), jax.random.fold_in(key_of[1], 1), 0, 1),
        "kernels": noise(key_of[2], (KERNELS, 2, KSIZE, KSIZE), (KSIZE * KSIZE) ** -0.5, 0.1875),
        "weights": jnp.clip(jnp.exp(jax.random.uniform(key_of[3], (KERNELS,), jnp.float32, math.log(0.2), math.log(1.0))), 0.2, 1.0),
        "doses": jnp.clip(jax.random.uniform(key_of[4], (CONDS,), jnp.float32, 0.8, 1.2), 0.8, 1.2),
        "site_pix": set_ends(jax.random.randint(key_of[5], (N_ROW * DEVICES, N_COL * CAP), 0, TILE_ROWS * TILE_COLS), jax.random.fold_in(key_of[5], 1), 0, (TILE_ROWS * TILE_COLS) - 1).astype(jnp.int32),
        "send_count": draw_send_count(jax.random.fold_in(key_of[9], 71), 0),
        "recv_frag": set_ends(jax.random.randint(key_of[7], (N_ROW * DEVICES, N_COL * CAP), 0, FRAGS), jax.random.fold_in(key_of[7], 1), 0, FRAGS - 1).astype(jnp.int32),
        "frag_target": jnp.clip(6.0 * jax.random.uniform(key_of[8], (CONDS, DEVICES * FRAGS), jnp.float32) ** shard_levels(key_of[8], (CONDS, DEVICES * FRAGS), ((1, 128),), -0.2, 0.2), 0.0, 6.0),
    }


def reference(mask, target, kernels, weights, doses, site_pix, send_count, recv_frag, frag_target):
    steepness = 4.0
    threshold = 1.2
    height = TILE_ROWS * N_ROW
    width_all = TILE_COLS * N_COL
    pad_rows = height + 64
    pad_cols = width_all + 256
    extent = kernels.shape[-1]
    reach = extent // 2
    kernel_taps = kernels.astype(jnp.float32).reshape(-1, extent, extent)
    field_gain = jnp.repeat(weights, 2)
    mask_hat = jnp.fft.rfft2(mask.astype(jnp.float32), s=(pad_rows, pad_cols))

    def spectrum(small):
        image = jnp.zeros((pad_rows, pad_cols), jnp.float32).at[:extent, :extent].set(small)
        image = jnp.roll(image, (-reach, -reach), axis=(0, 1))
        return jnp.fft.rfft2(image)

    def forward_field(index):
        full = jnp.fft.irfft2(mask_hat * spectrum(kernel_taps[index][::-1, ::-1]), s=(pad_rows, pad_cols))
        return full[:height, :width_all].astype(jnp.float32)

    intensity = jnp.zeros((height, width_all), jnp.float32)
    for index in range(kernel_taps.shape[0]):
        field = forward_field(index)
        intensity = intensity + field_gain[index] * field * field

    nominal = jax.nn.sigmoid(steepness * (intensity - threshold))
    dense = (nominal - target.astype(jnp.float32)) * steepness * nominal * (1.0 - nominal)

    sites = site_pix.reshape(N_ROW, DEVICES, N_COL, CAP).transpose(0, 2, 1, 3)
    row_base = (jnp.arange(N_ROW) * TILE_ROWS).astype(jnp.int32)[:, None, None, None]
    col_base = (jnp.arange(N_COL) * TILE_COLS).astype(jnp.int32)[None, :, None, None]
    rows_at = (row_base + sites // TILE_COLS).reshape(DEVICES, DEVICES, CAP)
    cols_at = (col_base + sites % TILE_COLS).reshape(DEVICES, DEVICES, CAP)
    level = intensity[rows_at, cols_at]
    counts = send_count.reshape(DEVICES, DEVICES)
    live = (jnp.arange(CAP)[None, None, :] < counts[:, :, None]).astype(jnp.float32)
    resist = jax.nn.sigmoid(steepness * (doses[:, None, None, None] * level[None] - threshold))
    value = resist * live[None]

    owner_frag = recv_frag.reshape(N_ROW, DEVICES, N_COL, CAP).transpose(0, 2, 1, 3).reshape(DEVICES, DEVICES, CAP)
    frag_ids = (jnp.arange(DEVICES)[:, None, None] * FRAGS + owner_frag).astype(jnp.int32)
    by_owner = value.transpose(0, 2, 1, 3).reshape(CONDS, -1)

    def add_sites(values_line):
        return jax.ops.segment_sum(values_line, frag_ids.reshape(-1), DEVICES * FRAGS)

    frag_error = jax.vmap(add_sites)(by_owner) - frag_target
    reply = frag_error[:, frag_ids].transpose(0, 2, 1, 3) * live[None]
    site_slope = jnp.sum(reply * steepness * doses[:, None, None, None] * resist * (1.0 - resist), axis=0)
    slope = dense.at[rows_at.reshape(-1), cols_at.reshape(-1)].add(site_slope.reshape(-1))

    gradient = jnp.zeros((height, width_all), jnp.float32)
    for index in range(kernel_taps.shape[0]):
        field = forward_field(index)
        weighted = lax.optimization_barrier((field_gain[index] * field * slope).astype(jnp.bfloat16))
        weighted = weighted.astype(jnp.float32)
        back = jnp.fft.irfft2(jnp.fft.rfft2(weighted, s=(pad_rows, pad_cols)) * spectrum(kernel_taps[index]), s=(pad_rows, pad_cols))
        gradient = gradient + 2.0 * back[:height, :width_all].astype(jnp.float32)
    return gradient, frag_error
```

```python
import functools

import jax
import jax.numpy as jnp
from jax import lax
from jax.experimental import pallas as pl
from jax.experimental.pallas import tpu as pltpu
from jax.sharding import PartitionSpec as P

steepness = 4.0
threshold = 1.2
f32 = jnp.float32
bf16 = jnp.bfloat16
LANES = 128
VMEM_BYTES = 48 << 20


def call(kernel, out_shapes, scratch=(), flops=0, moved=0, smem=(), inputs=0):
    vmem = pl.BlockSpec(memory_space=pltpu.VMEM)
    specs = [
        pl.BlockSpec(memory_space=pltpu.SMEM) if i in smem else vmem for i in range(inputs)
    ]
    return pl.pallas_call(
        kernel,
        out_shape=out_shapes,
        in_specs=specs,
        out_specs=jax.tree.map(lambda _: vmem, out_shapes),
        scratch_shapes=list(scratch),
        cost_estimate=pl.CostEstimate(flops=flops, bytes_accessed=moved, transcendentals=0),
        compiler_params=pltpu.CompilerParams(vmem_limit_bytes=VMEM_BYTES),
    )


def ring_halo(block, axis, dim, width):
    count = lax.axis_size(axis)
    index = lax.axis_index(axis)
    up = [(i, (i + 1) % count) for i in range(count)]
    down = [(target, source) for source, target in up]
    size = block.shape[dim]
    low = lax.ppermute(lax.slice_in_dim(block, size - width, size, axis=dim), axis, up)
    high = lax.ppermute(lax.slice_in_dim(block, 0, width, axis=dim), axis, down)
    zero = jnp.zeros((), block.dtype)
    low = jnp.where(index == 0, zero, low)
    high = jnp.where(index == count - 1, zero, high)
    return jnp.concatenate([low, block, high], axis=dim)


def shear(row, rows):
    wide = jnp.broadcast_to(row, (rows, row.shape[1]))
    return pltpu.roll(wide, 0, axis=1, stride=1, stride_axis=0)


def table_kernel(rows, lines_ref, out_ref):
    def one(index, carry):
        line = lines_ref[pl.ds(index, 1), :]
        start = pl.multiple_of(index * rows, rows)
        out_ref[pl.ds(start, rows), :] = shear(line, rows).astype(bf16)
        return carry

    lax.fori_loop(0, lines_ref.shape[0], one, 0)


def banded(lines, rows):
    count, width = lines.shape
    return call(
        functools.partial(table_kernel, rows),
        jax.ShapeDtypeStruct((count * rows, width), bf16),
        inputs=1,
        moved=2 * count * rows * width,
    )(lines)


def stack_shifts(plane, taps, first, out_ref):
    height, width = plane.shape
    columns = out_ref.shape[1]

    def one(v, carry):
        moved = pltpu.roll(plane, width - first - v, axis=1)[:, :columns]
        start = pl.multiple_of(v * height, height)
        out_ref[pl.ds(start, height), :] = moved.astype(bf16)
        return carry

    lax.fori_loop(0, taps, one, 0)
    rest = out_ref.shape[0] - taps * height
    out_ref[taps * height :, :] = jnp.zeros((rest, columns), bf16)


def forward_kernel(
    taps, reach, gain_ref, mask_ref, table_ref, pix_ref, count_ref, level_ref, inten_ref, stack_ref, lines_ref
):
    rows, columns = inten_ref.shape
    plane = mask_ref[reach : reach + rows + 2 * reach, :].astype(f32)
    stack_shifts(plane, taps, reach, stack_ref)
    fields = jnp.dot(table_ref[...], stack_ref[...], preferred_element_type=f32)
    total = jnp.zeros((rows, columns), f32)
    for k in range(gain_ref.shape[0]):
        real = fields[2 * k * rows : (2 * k + 1) * rows]
        imag = fields[(2 * k + 1) * rows : (2 * k + 2) * rows]
        total = total + gain_ref[k] * (real * real + imag * imag)
    inten_ref[...] = total
    halves = columns // LANES
    for half in range(halves):
        lines_ref[half * rows : (half + 1) * rows, :] = total[:, half * LANES : (half + 1) * LANES]
    pix = pix_ref[...]
    slots, owners = pix.shape
    low = pix & (LANES - 1)
    high = pix >> 7

    def pick(i, level):
        for half in range(halves):
            line = lines_ref[pl.ds(half * rows + i, 1), :]
            wide = jnp.broadcast_to(line, (slots, LANES))
            found = jnp.take_along_axis(wide, low, axis=1, mode="promise_in_bounds")
            level = jnp.where(high == i * halves + half, found, level)
        return level

    level = lax.fori_loop(0, rows, pick, jnp.zeros((slots, owners), f32))
    live = lax.broadcasted_iota(jnp.int32, (slots, owners), 0) < count_ref[...]
    level = jnp.where(live, level, -1.0)
    level = jnp.concatenate([level, jnp.zeros((owners - slots, owners), f32)], axis=0)
    level_ref[...] = level.T


def wide_kernel(taps, rows, chunk, mask_ref, lines_ref, fields_ref, table_ref, stack_ref):
    plane = mask_ref[...].astype(f32)
    stack_shifts(plane, taps, 0, stack_ref)
    table_kernel(rows, lines_ref, table_ref)
    count = table_ref.shape[0] // chunk

    def one(index, carry):
        start = pl.multiple_of(index * chunk, chunk)
        fields_ref[pl.ds(start, chunk), :] = jnp.dot(
            table_ref[pl.ds(start, chunk), :], stack_ref[...], preferred_element_type=f32
        )
        return carry

    lax.fori_loop(0, count, one, 0)


def split(x):
    top = x.astype(bf16)
    return top.astype(f32), x - top.astype(f32)


def one_hot(index, size):
    ids = lax.broadcasted_iota(jnp.int32, (size, LANES), 0)
    return jnp.where(ids == index, 1.0, 0.0).astype(bf16)


def product_nt(a, b):
    return lax.dot_general(a, b, (((1,), (1,)), ((), ())), preferred_element_type=f32)


def owner_kernel(dose_ref, level_ref, frag_ref, aim_ref, error_ref, slope_ref, level_t, slope_t):
    slots = frag_ref.shape[0]
    conds = dose_ref.shape[0]
    bins = aim_ref.shape[1] // LANES
    level_t[...] = level_ref[...].T
    dose = jnp.broadcast_to(dose_ref[...], (conds, LANES))

    def resist_of(c):
        level = jnp.broadcast_to(level_t[pl.ds(c, 1), :], (conds, LANES))
        return level, jax.nn.sigmoid(steepness * (dose * level - threshold))

    def add(pair, total):
        left, right = [], []
        for c in (2 * pair, 2 * pair + 1):
            level, resist = resist_of(c)
            frag = jnp.broadcast_to(frag_ref[pl.ds(c, 1), :], (conds, LANES))
            top, rest = split(jnp.where(level >= 0.0, resist, 0.0))
            bin_of = frag >> 7
            left.append(
                jnp.concatenate(
                    [jnp.where(bin_of == q, part, 0.0) for part in (top, rest) for q in range(bins)],
                    axis=0,
                ).astype(bf16)
            )
            right.append(one_hot(frag_ref[pl.ds(c, 1), :] & (LANES - 1), LANES))
        return total + product_nt(
            jnp.concatenate(left, axis=1), jnp.concatenate(right, axis=1)
        )

    total = lax.fori_loop(0, slots // 2, add, jnp.zeros((2 * bins * conds, LANES), f32))
    total = total[: bins * conds] + total[bins * conds :]
    for q in range(bins):
        lanes = slice(q * LANES, (q + 1) * LANES)
        error_ref[:, lanes] = total[q * conds : (q + 1) * conds] - aim_ref[:, lanes]

    def answer(c, carry):
        level, resist = resist_of(c)
        frag = jnp.broadcast_to(frag_ref[pl.ds(c, 1), :], (conds, LANES))
        low = frag & (LANES - 1)
        bin_of = frag >> 7
        reply = jnp.zeros((conds, LANES), f32)
        for q in range(bins):
            found = jnp.take_along_axis(
                error_ref[:, q * LANES : (q + 1) * LANES], low, axis=1, mode="promise_in_bounds"
            )
            reply = jnp.where(bin_of == q, found, reply)
        terms = reply * steepness * dose * resist * (1.0 - resist)
        terms = jnp.where(level >= 0.0, terms, 0.0)
        slope_t[pl.ds(c, 1), :] = jnp.sum(terms, axis=0, keepdims=True)
        return carry

    lax.fori_loop(0, slots, answer, 0)
    slope_t[slots:, :] = jnp.zeros((LANES - slots, LANES), f32)
    slope_ref[...] = slope_t[...].T


def site_kernel(reply_ref, pix_ref, inten_ref, target_ref, slope_ref, reply_t):
    rows, columns = inten_ref.shape
    slots = pix_ref.shape[0]
    halves = columns // LANES
    reply_t[...] = reply_ref[...].T

    def add(pair, total):
        left, right = [], []
        for c in (2 * pair, 2 * pair + 1):
            pix = pix_ref[pl.ds(c, 1), :]
            line = pix >> 7
            line = (line % halves) * rows + line // halves
            ids = lax.broadcasted_iota(jnp.int32, (rows * halves, LANES), 0)
            top, rest = split(reply_t[pl.ds(c, 1), :])
            here = ids == line
            left.append(
                jnp.concatenate(
                    [jnp.where(here, top, 0.0), jnp.where(here, rest, 0.0)], axis=0
                ).astype(bf16)
            )
            right.append(one_hot(pix & (LANES - 1), LANES))
        return total + product_nt(
            jnp.concatenate(left, axis=1), jnp.concatenate(right, axis=1)
        )

    size = rows * halves
    total = lax.fori_loop(0, slots // 2, add, jnp.zeros((2 * size, LANES), f32))
    total = total[:size] + total[size:]
    for half in range(halves):
        lanes = slice(half * LANES, (half + 1) * LANES)
        nominal = jax.nn.sigmoid(steepness * (inten_ref[:, lanes] - threshold))
        gap = nominal - target_ref[:, lanes].astype(f32)
        dense = gap * steepness * nominal * (1.0 - nominal)
        slope_ref[:, lanes] = dense + total[half * rows : (half + 1) * rows]


def back_kernel(taps, gain_ref, fields_ref, slope_ref, table_ref, out_ref, weighted_ref, part_ref):
    rows, columns = out_ref.shape
    height, width = slope_ref.shape
    slope = slope_ref[...]

    def weigh(h, carry):
        start = pl.multiple_of(h * height, height)
        field = fields_ref[pl.ds(start, height), :]
        weighted_ref[pl.ds(start, height), :] = (gain_ref[h // 2] * field * slope).astype(bf16)
        return carry

    lax.fori_loop(0, weighted_ref.shape[0] // height, weigh, 0)
    part_ref[...] = jnp.dot(table_ref[...], weighted_ref[...], preferred_element_type=f32)

    def gather(v, total):
        start = pl.multiple_of(v * rows, rows)
        return total + pltpu.roll(part_ref[pl.ds(start, rows), :], width - v, axis=1)[:, :columns]

    total = lax.fori_loop(0, taps, gather, jnp.zeros((rows, columns), f32))
    out_ref[...] = 2.0 * total


def round_up(x, to):
    return -(-x // to) * to


def lines_of(taps, stride, length):
    count, blocks, extent = taps.shape
    padded = jnp.pad(taps, ((0, 0), (0, 0), (0, stride - extent)))
    flat = padded.reshape(count, blocks * stride)
    return jnp.pad(flat, ((0, 0), (0, length - blocks * stride))).astype(f32)


def body(mask, target, kernels, weights, doses, site_pix, send_count, recv_frag, frag_target):
    rows, columns = mask.shape
    extent = kernels.shape[-1]
    reach = extent // 2
    kernel_taps = kernels.reshape(-1, extent, extent)
    parts = kernel_taps.shape[0]
    owners = site_pix.shape[0]
    both = ("row", "col")

    near = ring_halo(mask, "row", 0, 2 * reach)
    near = ring_halo(near, "col", 1, 2 * reach)
    wide_columns = round_up(near.shape[1], LANES)
    near = jnp.pad(near, ((0, 0), (0, wide_columns - near.shape[1])))

    height = rows + 2 * reach
    by_column = kernel_taps.transpose(0, 2, 1)
    core_depth = round_up(extent * height, LANES)
    core_table = banded(lines_of(by_column, height, core_depth), rows)

    pix = site_pix.T
    level, intensity = call(
        functools.partial(forward_kernel, extent, reach),
        (
            jax.ShapeDtypeStruct((owners, LANES), f32),
            jax.ShapeDtypeStruct((rows, columns), f32),
        ),
        scratch=[
            pltpu.VMEM((core_depth, columns), bf16),
            pltpu.VMEM((rows * columns // LANES, LANES), f32),
        ],
        inputs=5,
        smem=(0,),
        flops=2 * parts * rows * core_depth * columns,
        moved=2 * parts * rows * core_depth,
    )(weights, near, core_table, pix, send_count)

    level, near = lax.optimization_barrier((level, near))
    arrived = lax.all_to_all(level, both, split_axis=0, concat_axis=0, tiled=True)

    tall = rows + 4 * reach
    wide_depth = round_up(extent * tall, LANES)
    wide_fields = call(
        functools.partial(wide_kernel, extent, height, 256),
        jax.ShapeDtypeStruct((parts * height, wide_columns), f32),
        scratch=[
            pltpu.VMEM((parts * height, wide_depth), bf16),
            pltpu.VMEM((wide_depth, wide_columns), bf16),
        ],
        inputs=2,
        flops=2 * parts * height * wide_depth * wide_columns,
        moved=4 * parts * height * wide_columns,
    )(near, lines_of(by_column, tall, wide_depth))

    arrived, wide_fields = lax.optimization_barrier((arrived, wide_fields))

    frag_error, answers = call(
        owner_kernel,
        (
            jax.ShapeDtypeStruct(frag_target.shape, f32),
            jax.ShapeDtypeStruct((owners, LANES), f32),
        ),
        scratch=[pltpu.VMEM((LANES, LANES), f32)] * 2,
        inputs=4,
        flops=2 * 2 * frag_target.size * site_pix.size // 16,
        moved=8 * frag_target.size,
    )(doses[:, None], arrived, recv_frag.T, frag_target)

    flipped = kernel_taps[:, ::-1, ::-1].transpose(2, 0, 1)
    back_depth = parts * height
    back_lines = lines_of(flipped, height, back_depth)
    answers, back_lines = lax.optimization_barrier((answers, back_lines))
    returned = lax.all_to_all(answers, both, split_axis=0, concat_axis=0, tiled=True)
    back_table = banded(back_lines, rows)
    returned, back_table = lax.optimization_barrier((returned, back_table))
    slope = call(
        site_kernel,
        jax.ShapeDtypeStruct((rows, columns), f32),
        scratch=[pltpu.VMEM((LANES, LANES), f32)],
        inputs=4,
        flops=2 * 2 * rows * columns * site_pix.size // 64,
        moved=16 * rows * columns,
    )(returned, pix, intensity, target)

    around = ring_halo(slope, "row", 0, reach)
    around = ring_halo(around, "col", 1, reach)
    around = jnp.pad(around, ((0, 0), (0, wide_columns - around.shape[1])))
    gradient = call(
        functools.partial(back_kernel, extent),
        jax.ShapeDtypeStruct((rows, columns), f32),
        scratch=[
            pltpu.VMEM((back_depth, wide_columns), bf16),
            pltpu.VMEM((extent * rows, wide_columns), f32),
        ],
        inputs=4,
        smem=(0,),
        flops=2 * extent * rows * back_depth * wide_columns,
        moved=8 * back_depth * wide_columns,
    )(weights, wide_fields, around, back_table)
    return gradient, frag_error


def solution(mesh):
    return jax.shard_map(
        body,
        mesh=mesh,
        in_specs=(
            P("row", "col"),
            P("row", "col"),
            P(),
            P(),
            P(),
            P("row", "col"),
            P("row", "col"),
            P("row", "col"),
            P(None, ("row", "col")),
        ),
        out_specs=(P("row", "col"), P(None, ("row", "col"))),
        check_vma=False,
    )
```

```python
import functools

import jax
import jax.numpy as jnp
from jax import lax
from jax.experimental import pallas as pl
from jax.experimental.pallas import tpu as pltpu
from jax.sharding import PartitionSpec as P

steepness = 4.0
threshold = 1.2
f32 = jnp.float32
bf16 = jnp.bfloat16
LANES = 128
VMEM_BYTES = 48 << 20
UNROLL = {
    "table": 4,
    "stack": 33,
    "pick": 32,
    "wide": 1,
    "owner": 4,
    "answer": 16,
    "site": 4,
    "weigh": 16,
    "gather": 33,
}


def call(kernel, out_shapes, scratch=(), flops=0, moved=0, smem=(), inputs=0):
    vmem = pl.BlockSpec(memory_space=pltpu.VMEM)
    specs = [
        pl.BlockSpec(memory_space=pltpu.SMEM) if i in smem else vmem for i in range(inputs)
    ]
    return pl.pallas_call(
        kernel,
        out_shape=out_shapes,
        in_specs=specs,
        out_specs=jax.tree.map(lambda _: vmem, out_shapes),
        scratch_shapes=list(scratch),
        cost_estimate=pl.CostEstimate(flops=flops, bytes_accessed=moved, transcendentals=0),
        compiler_params=pltpu.CompilerParams(vmem_limit_bytes=VMEM_BYTES),
    )


def ring_halo(block, axis, dim, width):
    count = lax.axis_size(axis)
    index = lax.axis_index(axis)
    up = [(i, (i + 1) % count) for i in range(count)]
    down = [(target, source) for source, target in up]
    size = block.shape[dim]
    low = lax.ppermute(lax.slice_in_dim(block, size - width, size, axis=dim), axis, up)
    high = lax.ppermute(lax.slice_in_dim(block, 0, width, axis=dim), axis, down)
    zero = jnp.zeros((), block.dtype)
    low = jnp.where(index == 0, zero, low)
    high = jnp.where(index == count - 1, zero, high)
    return jnp.concatenate([low, block, high], axis=dim)


def shear(row, rows):
    wide = jnp.broadcast_to(row, (rows, row.shape[1]))
    return pltpu.roll(wide, 0, axis=1, stride=1, stride_axis=0)


def table_kernel(rows, lines_ref, out_ref):
    def one(index, carry):
        line = lines_ref[pl.ds(index, 1), :]
        start = pl.multiple_of(index * rows, rows)
        out_ref[pl.ds(start, rows), :] = shear(line, rows).astype(bf16)
        return carry

    lax.fori_loop(0, lines_ref.shape[0], one, 0, unroll=UNROLL["table"])


def banded(lines, rows):
    count, width = lines.shape
    return call(
        functools.partial(table_kernel, rows),
        jax.ShapeDtypeStruct((count * rows, width), bf16),
        inputs=1,
        moved=2 * count * rows * width,
    )(lines)


def stack_shifts(plane, taps, first, out_ref):
    height, width = plane.shape
    columns = out_ref.shape[1]

    def one(v, carry):
        moved = pltpu.roll(plane, width - first - v, axis=1)[:, :columns]
        start = pl.multiple_of(v * height, height)
        out_ref[pl.ds(start, height), :] = moved.astype(bf16)
        return carry

    lax.fori_loop(0, taps, one, 0, unroll=UNROLL["stack"])
    rest = out_ref.shape[0] - taps * height
    out_ref[taps * height :, :] = jnp.zeros((rest, columns), bf16)


def forward_kernel(
    taps, reach, gain_ref, mask_ref, table_ref, pix_ref, count_ref, level_ref, inten_ref, stack_ref, lines_ref
):
    rows, columns = inten_ref.shape
    plane = mask_ref[reach : reach + rows + 2 * reach, :].astype(f32)
    stack_shifts(plane, taps, reach, stack_ref)
    fields = jnp.dot(table_ref[...], stack_ref[...], preferred_element_type=f32)
    total = jnp.zeros((rows, columns), f32)
    for k in range(gain_ref.shape[0]):
        real = fields[2 * k * rows : (2 * k + 1) * rows]
        imag = fields[(2 * k + 1) * rows : (2 * k + 2) * rows]
        total = total + gain_ref[k] * (real * real + imag * imag)
    inten_ref[...] = total
    halves = columns // LANES
    for half in range(halves):
        lines_ref[half * rows : (half + 1) * rows, :] = total[:, half * LANES : (half + 1) * LANES]
    pix = pix_ref[...]
    slots, owners = pix.shape
    low = pix & (LANES - 1)
    high = pix >> 7

    def pick(i, level):
        for half in range(halves):
            line = lines_ref[pl.ds(half * rows + i, 1), :]
            wide = jnp.broadcast_to(line, (slots, LANES))
            found = jnp.take_along_axis(wide, low, axis=1, mode="promise_in_bounds")
            level = jnp.where(high == i * halves + half, found, level)
        return level

    level = lax.fori_loop(0, rows, pick, jnp.zeros((slots, owners), f32), unroll=UNROLL["pick"])
    live = lax.broadcasted_iota(jnp.int32, (slots, owners), 0) < count_ref[...]
    level = jnp.where(live, level, -1.0)
    level = jnp.concatenate([level, jnp.zeros((owners - slots, owners), f32)], axis=0)
    level_ref[...] = level.T


def wide_kernel(taps, rows, chunk, mask_ref, lines_ref, fields_ref, table_ref, stack_ref):
    plane = mask_ref[...].astype(f32)
    stack_shifts(plane, taps, 0, stack_ref)
    table_kernel(rows, lines_ref, table_ref)
    count = table_ref.shape[0] // chunk

    def one(index, carry):
        start = pl.multiple_of(index * chunk, chunk)
        fields_ref[pl.ds(start, chunk), :] = jnp.dot(
            table_ref[pl.ds(start, chunk), :], stack_ref[...], preferred_element_type=f32
        )
        return carry

    lax.fori_loop(0, count, one, 0, unroll=UNROLL["wide"])


def split(x):
    top = x.astype(bf16)
    return top.astype(f32), x - top.astype(f32)


def one_hot(index, size):
    ids = lax.broadcasted_iota(jnp.int32, (size, LANES), 0)
    return jnp.where(ids == index, 1.0, 0.0).astype(bf16)


def product_nt(a, b):
    return lax.dot_general(a, b, (((1,), (1,)), ((), ())), preferred_element_type=f32)


def side_by_side(ref):
    return jnp.concatenate([ref[c] for c in range(ref.shape[0])], axis=1)


def owner_kernel(
    dose_ref,
    level_ref,
    frag_ref,
    aim_ref,
    error_ref,
    slope_ref,
    level_t,
    slope_t,
    resist_ref,
    value_ref,
    place_ref,
):
    slots = frag_ref.shape[0]
    conds = dose_ref.shape[0]
    bins = aim_ref.shape[1] // LANES
    level_t[...] = level_ref[...].T
    dose = jnp.broadcast_to(dose_ref[...], (conds, LANES))

    def place(c, carry):
        level = jnp.broadcast_to(level_t[pl.ds(c, 1), :], (conds, LANES))
        resist = jax.nn.sigmoid(steepness * (dose * level - threshold))
        live = level >= 0.0
        resist_ref[c] = jnp.where(live, resist, 0.0)
        top, rest = split(jnp.where(live, resist, 0.0))
        frag = frag_ref[pl.ds(c, 1), :]
        bin_of = jnp.broadcast_to(frag >> 7, (conds, LANES))
        value_ref[c] = jnp.concatenate(
            [jnp.where(bin_of == q, part, 0.0) for part in (top, rest) for q in range(bins)],
            axis=0,
        ).astype(bf16)
        place_ref[c] = one_hot(frag & (LANES - 1), LANES)
        return carry

    lax.fori_loop(0, slots, place, 0, unroll=UNROLL["owner"])
    total = product_nt(side_by_side(value_ref), side_by_side(place_ref))
    total = total[: bins * conds] + total[bins * conds :]
    for q in range(bins):
        lanes = slice(q * LANES, (q + 1) * LANES)
        error_ref[:, lanes] = total[q * conds : (q + 1) * conds] - aim_ref[:, lanes]

    def answer(c, carry):
        resist = resist_ref[c]
        frag = jnp.broadcast_to(frag_ref[pl.ds(c, 1), :], (conds, LANES))
        low = frag & (LANES - 1)
        bin_of = frag >> 7
        reply = jnp.zeros((conds, LANES), f32)
        for q in range(bins):
            found = jnp.take_along_axis(
                error_ref[:, q * LANES : (q + 1) * LANES], low, axis=1, mode="promise_in_bounds"
            )
            reply = jnp.where(bin_of == q, found, reply)
        terms = reply * steepness * dose * resist * (1.0 - resist)
        slope_t[pl.ds(c, 1), :] = jnp.sum(terms, axis=0, keepdims=True)
        return carry

    lax.fori_loop(0, slots, answer, 0, unroll=UNROLL["answer"])
    slope_t[slots:, :] = jnp.zeros((LANES - slots, LANES), f32)
    slope_ref[...] = slope_t[...].T


def site_kernel(
    reply_ref, pix_ref, inten_ref, target_ref, slope_ref, reply_t, value_ref, place_ref
):
    rows, columns = inten_ref.shape
    slots = pix_ref.shape[0]
    halves = columns // LANES
    size = rows * halves
    reply_t[...] = reply_ref[...].T

    def place(c, carry):
        pix = pix_ref[pl.ds(c, 1), :]
        line = pix >> 7
        line = (line % halves) * rows + line // halves
        here = lax.broadcasted_iota(jnp.int32, (size, LANES), 0) == line
        top, rest = split(reply_t[pl.ds(c, 1), :])
        value_ref[c] = jnp.concatenate(
            [jnp.where(here, top, 0.0), jnp.where(here, rest, 0.0)], axis=0
        ).astype(bf16)
        place_ref[c] = one_hot(pix & (LANES - 1), LANES)
        return carry

    lax.fori_loop(0, slots, place, 0, unroll=UNROLL["site"])
    total = product_nt(side_by_side(value_ref), side_by_side(place_ref))
    total = total[:size] + total[size:]
    for half in range(halves):
        lanes = slice(half * LANES, (half + 1) * LANES)
        nominal = jax.nn.sigmoid(steepness * (inten_ref[:, lanes] - threshold))
        gap = nominal - target_ref[:, lanes].astype(f32)
        dense = gap * steepness * nominal * (1.0 - nominal)
        slope_ref[:, lanes] = dense + total[half * rows : (half + 1) * rows]


def back_kernel(taps, gain_ref, fields_ref, slope_ref, table_ref, out_ref, weighted_ref, part_ref):
    rows, columns = out_ref.shape
    height, width = slope_ref.shape
    slope = slope_ref[...]

    def weigh(h, carry):
        start = pl.multiple_of(h * height, height)
        field = fields_ref[pl.ds(start, height), :]
        weighted_ref[pl.ds(start, height), :] = (gain_ref[h // 2] * field * slope).astype(bf16)
        return carry

    lax.fori_loop(0, weighted_ref.shape[0] // height, weigh, 0, unroll=UNROLL["weigh"])
    part_ref[...] = jnp.dot(table_ref[...], weighted_ref[...], preferred_element_type=f32)

    def gather(v, total):
        start = pl.multiple_of(v * rows, rows)
        return total + pltpu.roll(part_ref[pl.ds(start, rows), :], width - v, axis=1)[:, :columns]

    total = lax.fori_loop(0, taps, gather, jnp.zeros((rows, columns), f32), unroll=UNROLL["gather"])
    out_ref[...] = 2.0 * total


def round_up(x, to):
    return -(-x // to) * to


def lines_of(taps, stride, length):
    count, blocks, extent = taps.shape
    padded = jnp.pad(taps, ((0, 0), (0, 0), (0, stride - extent)))
    flat = padded.reshape(count, blocks * stride)
    return jnp.pad(flat, ((0, 0), (0, length - blocks * stride))).astype(f32)


def body(mask, target, kernels, weights, doses, site_pix, send_count, recv_frag, frag_target):
    rows, columns = mask.shape
    extent = kernels.shape[-1]
    reach = extent // 2
    kernel_taps = kernels.reshape(-1, extent, extent)
    parts = kernel_taps.shape[0]
    owners, slots = site_pix.shape
    conds = doses.shape[0]
    both = ("row", "col")

    near = ring_halo(mask, "row", 0, 2 * reach)
    near = ring_halo(near, "col", 1, 2 * reach)
    wide_columns = round_up(near.shape[1], LANES)
    near = jnp.pad(near, ((0, 0), (0, wide_columns - near.shape[1])))

    height = rows + 2 * reach
    by_column = kernel_taps.transpose(0, 2, 1)
    core_depth = round_up(extent * height, LANES)
    core_table = banded(lines_of(by_column, height, core_depth), rows)

    pix = site_pix.T
    level, intensity = call(
        functools.partial(forward_kernel, extent, reach),
        (
            jax.ShapeDtypeStruct((owners, LANES), f32),
            jax.ShapeDtypeStruct((rows, columns), f32),
        ),
        scratch=[
            pltpu.VMEM((core_depth, columns), bf16),
            pltpu.VMEM((rows * columns // LANES, LANES), f32),
        ],
        inputs=5,
        smem=(0,),
        flops=2 * parts * rows * core_depth * columns,
        moved=2 * parts * rows * core_depth,
    )(weights, near, core_table, pix, send_count)

    level, near = lax.optimization_barrier((level, near))
    arrived = lax.all_to_all(level, both, split_axis=0, concat_axis=0, tiled=True)

    tall = rows + 4 * reach
    wide_depth = round_up(extent * tall, LANES)
    wide_fields = call(
        functools.partial(wide_kernel, extent, height, 512),
        jax.ShapeDtypeStruct((parts * height, wide_columns), f32),
        scratch=[
            pltpu.VMEM((parts * height, wide_depth), bf16),
            pltpu.VMEM((wide_depth, wide_columns), bf16),
        ],
        inputs=2,
        flops=2 * parts * height * wide_depth * wide_columns,
        moved=4 * parts * height * wide_columns,
    )(near, lines_of(by_column, tall, wide_depth))

    arrived, wide_fields = lax.optimization_barrier((arrived, wide_fields))

    frag_error, answers = call(
        owner_kernel,
        (
            jax.ShapeDtypeStruct(frag_target.shape, f32),
            jax.ShapeDtypeStruct((owners, LANES), f32),
        ),
        scratch=[
            pltpu.VMEM((LANES, LANES), f32),
            pltpu.VMEM((LANES, LANES), f32),
            pltpu.VMEM((slots, conds, LANES), f32),
            pltpu.VMEM((slots, 2 * frag_target.size // LANES, LANES), bf16),
            pltpu.VMEM((slots, LANES, LANES), bf16),
        ],
        inputs=4,
        flops=2 * 2 * frag_target.size * site_pix.size // 16,
        moved=8 * frag_target.size,
    )(doses[:, None], arrived, recv_frag.T, frag_target)

    flipped = kernel_taps[:, ::-1, ::-1].transpose(2, 0, 1)
    back_depth = parts * height
    back_lines = lines_of(flipped, height, back_depth)
    answers, back_lines = lax.optimization_barrier((answers, back_lines))
    returned = lax.all_to_all(answers, both, split_axis=0, concat_axis=0, tiled=True)
    back_table = banded(back_lines, rows)
    returned, back_table = lax.optimization_barrier((returned, back_table))
    slope = call(
        site_kernel,
        jax.ShapeDtypeStruct((rows, columns), f32),
        scratch=[
            pltpu.VMEM((LANES, LANES), f32),
            pltpu.VMEM((slots, 2 * rows * columns // LANES, LANES), bf16),
            pltpu.VMEM((slots, LANES, LANES), bf16),
        ],
        inputs=4,
        flops=2 * 2 * rows * columns * site_pix.size // 64,
        moved=16 * rows * columns,
    )(returned, pix, intensity, target)

    around = ring_halo(slope, "row", 0, reach)
    around = ring_halo(around, "col", 1, reach)
    around = jnp.pad(around, ((0, 0), (0, wide_columns - around.shape[1])))
    gradient = call(
        functools.partial(back_kernel, extent),
        jax.ShapeDtypeStruct((rows, columns), f32),
        scratch=[
            pltpu.VMEM((back_depth, wide_columns), bf16),
            pltpu.VMEM((extent * rows, wide_columns), f32),
        ],
        inputs=4,
        smem=(0,),
        flops=2 * extent * rows * back_depth * wide_columns,
        moved=8 * back_depth * wide_columns,
    )(weights, wide_fields, around, back_table)
    return gradient, frag_error


def solution(mesh):
    return jax.shard_map(
        body,
        mesh=mesh,
        in_specs=(
            P("row", "col"),
            P("row", "col"),
            P(),
            P(),
            P(),
            P("row", "col"),
            P("row", "col"),
            P("row", "col"),
            P(None, ("row", "col")),
        ),
        out_specs=(P("row", "col"), P(None, ("row", "col"))),
        check_vma=False,
    )
```

```python
import functools

import jax
import jax.numpy as jnp
from jax import lax
from jax.experimental import pallas as pl
from jax.experimental.pallas import tpu as pltpu
from jax.sharding import PartitionSpec as P

steepness = 4.0
threshold = 1.2
f32 = jnp.float32
bf16 = jnp.bfloat16
LANES = 128
NEIGHBOURS = [(down, right) for right in (-1, 0, 1) for down in (-1, 0, 1)]
MIB = 1 << 20
UNROLL = {
    "table": 4,
    "stack": 33,
    "pick": 32,
    "owner": 4,
    "answer": 16,
    "site": 4,
    "weigh": 16,
    "gather": 33,
}


def call(
    kernel, out_shapes, scratch=(), flops=0, moved=0, smem=(), hbm=(), hbm_out=(), inputs=0, vmem_mib=16
):
    vmem = pl.BlockSpec(memory_space=pltpu.VMEM)
    specs = [vmem] * inputs
    for i in smem:
        specs[i] = pl.BlockSpec(memory_space=pltpu.SMEM)
    for i in hbm:
        specs[i] = pl.BlockSpec(memory_space=pltpu.HBM)
    out_specs = jax.tree.map(lambda _: vmem, out_shapes)
    if hbm_out:
        out_specs = tuple(
            pl.BlockSpec(memory_space=pltpu.HBM) if i in hbm_out else vmem
            for i in range(len(out_shapes))
        )
    return pl.pallas_call(
        kernel,
        out_shape=out_shapes,
        in_specs=specs,
        out_specs=out_specs,
        scratch_shapes=list(scratch),
        cost_estimate=pl.CostEstimate(flops=flops, bytes_accessed=moved, transcendentals=0),
        compiler_params=pltpu.CompilerParams(vmem_limit_bytes=vmem_mib * MIB),
    )


def ring(low_end, high_end, axis):
    count = lax.axis_size(axis)
    up = [(i, (i + 1) % count) for i in range(count)]
    down = [(target, source) for source, target in up]
    return lax.ppermute(high_end, axis, up), lax.ppermute(low_end, axis, down)


def clipped(low, high, axis):
    index = lax.axis_index(axis)
    zero = jnp.zeros((), low.dtype)
    low = jnp.where(index == 0, zero, low)
    return low, jnp.where(index == lax.axis_size(axis) - 1, zero, high)


def shear(row, rows):
    wide = jnp.broadcast_to(row, (rows, row.shape[1]))
    return pltpu.roll(wide, 0, axis=1, stride=1, stride_axis=0)


def table_kernel(rows, lines_ref, out_ref):
    def one(index, carry):
        line = lines_ref[pl.ds(index, 1), :]
        start = pl.multiple_of(index * rows, rows)
        out_ref[pl.ds(start, rows), :] = shear(line, rows).astype(bf16)
        return carry

    lax.fori_loop(0, lines_ref.shape[0], one, 0, unroll=UNROLL["table"])


def banded(lines, rows, hbm=False):
    count, width = lines.shape
    return call(
        functools.partial(table_kernel, rows),
        jax.ShapeDtypeStruct((count * rows, width), bf16),
        inputs=1,
        moved=2 * count * rows * width,
    )(lines)


def stack_shifts(plane, taps, first, out_ref):
    height, width = plane.shape
    columns = out_ref.shape[1]

    def one(v, carry):
        moved = pltpu.roll(plane, width - first - v, axis=1)[:, :columns]
        start = pl.multiple_of(v * height, height)
        out_ref[pl.ds(start, height), :] = moved.astype(bf16)
        return carry

    lax.fori_loop(0, taps, one, 0, unroll=UNROLL["stack"])
    rest = out_ref.shape[0] - taps * height
    out_ref[taps * height :, :] = jnp.zeros((rest, columns), bf16)


def forward_kernel(
    taps, reach, gain_ref, mask_ref, table_ref, pix_ref, count_ref, level_ref, stack_ref, lines_ref
):
    columns = stack_ref.shape[1]
    halves = columns // LANES
    rows = lines_ref.shape[0] // halves
    plane = mask_ref[reach : reach + rows + 2 * reach, :].astype(f32)
    stack_shifts(plane, taps, reach, stack_ref)
    fields = jnp.dot(table_ref[...], stack_ref[...], preferred_element_type=f32)
    total = jnp.zeros((rows, columns), f32)
    for k in range(gain_ref.shape[0]):
        real = fields[2 * k * rows : (2 * k + 1) * rows]
        imag = fields[(2 * k + 1) * rows : (2 * k + 2) * rows]
        total = total + gain_ref[k] * (real * real + imag * imag)
    for half in range(halves):
        lines_ref[half * rows : (half + 1) * rows, :] = total[:, half * LANES : (half + 1) * LANES]
    pix = pix_ref[...]
    slots, owners = pix.shape
    low = pix & (LANES - 1)
    high = pix >> 7

    def pick(i, level):
        for half in range(halves):
            line = lines_ref[pl.ds(half * rows + i, 1), :]
            wide = jnp.broadcast_to(line, (slots, LANES))
            found = jnp.take_along_axis(wide, low, axis=1, mode="promise_in_bounds")
            level = jnp.where(high == i * halves + half, found, level)
        return level

    level = lax.fori_loop(0, rows, pick, jnp.zeros((slots, owners), f32), unroll=UNROLL["pick"])
    live = lax.broadcasted_iota(jnp.int32, (slots, owners), 0) < count_ref[...]
    level = jnp.where(live, level, -1.0)
    level = jnp.concatenate([level, jnp.zeros((owners - slots, owners), f32)], axis=0)
    level_ref[...] = level.T


def wide_kernel(
    taps,
    rows,
    chunk,
    gain_ref,
    near_ref,
    lines_ref,
    fields_hbm,
    inten_ref,
    fields_ref,
    table_ref,
    stack_ref,
    sems,
):
    plane = near_ref[...].astype(f32)
    stack_shifts(plane, taps, 0, stack_ref)
    table_kernel(rows, lines_ref, table_ref)
    copies = []
    for index in range(table_ref.shape[0] // chunk):
        part = pl.ds(index * chunk, chunk)
        fields_ref[part, :] = jnp.dot(
            table_ref[part, :], stack_ref[...], preferred_element_type=f32
        )
        copies.append(
            pltpu.make_async_copy(fields_ref.at[part], fields_hbm.at[part], sems.at[index])
        )
        copies[-1].start()
    total = jnp.zeros(inten_ref.shape, f32)
    for k in range(gain_ref.shape[0]):
        real = fields_ref[2 * k * rows : (2 * k + 1) * rows, :]
        imag = fields_ref[(2 * k + 1) * rows : (2 * k + 2) * rows, :]
        total = total + gain_ref[k] * (real * real + imag * imag)
    inten_ref[...] = total
    for copy in copies:
        copy.wait()


def spread(value, index, size):
    here = lax.broadcasted_iota(jnp.int32, (size, LANES), 0) == index
    return jnp.where(here, value, 0.0).astype(bf16)


def product_nt(a, b):
    return lax.dot_general(a, b, (((1,), (1,)), ((), ())), preferred_element_type=f32)


def side_by_side(ref):
    return jnp.concatenate([ref[c] for c in range(ref.shape[0])], axis=1)


def owner_kernel(
    grid_rows,
    grid_cols,
    dose_ref,
    level_ref,
    frag_ref,
    aim_ref,
    error_ref,
    slope_ref,
    level_t,
    slope_t,
    resist_ref,
    value_ref,
    place_ref,
    around_t,
):
    slots = frag_ref.shape[0]
    conds = dose_ref.shape[0]
    bins = aim_ref.shape[1] // LANES
    level_t[...] = level_ref[...].T
    dose = jnp.broadcast_to(dose_ref[...], (conds, LANES))

    def place(c, carry):
        level = jnp.broadcast_to(level_t[pl.ds(c, 1), :], (conds, LANES))
        resist = jax.nn.sigmoid(steepness * (dose * level - threshold))
        live = level >= 0.0
        resist_ref[c] = jnp.where(live, resist, 0.0)
        frag = frag_ref[pl.ds(c, 1), :]
        bin_of = jnp.broadcast_to(frag >> 7, (conds, LANES))
        value_ref[c] = jnp.concatenate(
            [jnp.where(bin_of == q, resist_ref[c], 0.0) for q in range(bins)], axis=0
        ).astype(bf16)
        place_ref[c] = spread(1.0, frag & (LANES - 1), LANES)
        return carry

    lax.fori_loop(0, slots, place, 0, unroll=UNROLL["owner"])
    total = product_nt(side_by_side(value_ref), side_by_side(place_ref))
    for q in range(bins):
        lanes = slice(q * LANES, (q + 1) * LANES)
        error_ref[:, lanes] = total[q * conds : (q + 1) * conds] - aim_ref[:, lanes]

    def answer(c, carry):
        resist = resist_ref[c]
        frag = jnp.broadcast_to(frag_ref[pl.ds(c, 1), :], (conds, LANES))
        low = frag & (LANES - 1)
        bin_of = frag >> 7
        reply = jnp.zeros((conds, LANES), f32)
        for q in range(bins):
            found = jnp.take_along_axis(
                error_ref[:, q * LANES : (q + 1) * LANES], low, axis=1, mode="promise_in_bounds"
            )
            reply = jnp.where(bin_of == q, found, reply)
        terms = reply * steepness * dose * resist * (1.0 - resist)
        slope_t[pl.ds(c, 1), :] = jnp.sum(terms, axis=0, keepdims=True)
        return carry

    lax.fori_loop(0, slots, answer, 0, unroll=UNROLL["answer"])
    slope = slope_t[:slots, :]
    lane = lax.broadcasted_iota(jnp.int32, (slots, LANES), 1)
    tile_row, tile_col = lane // grid_cols, lane % grid_cols
    for t, (down, right) in enumerate(NEIGHBOURS):
        row, col = tile_row + down, tile_col + right
        inside = (row >= 0) & (row < grid_rows) & (col >= 0) & (col < grid_cols)
        moved = pltpu.roll(slope, -(down * grid_cols + right) % LANES, axis=1)
        around_t[t * slots : (t + 1) * slots, :] = jnp.where(inside, moved, 0.0)
    rest = around_t.shape[0] - len(NEIGHBOURS) * slots
    around_t[len(NEIGHBOURS) * slots :, :] = jnp.zeros((rest, LANES), f32)
    for block in range(around_t.shape[0] // LANES):
        slope_ref[:, block, :] = around_t[block * LANES : (block + 1) * LANES, :].T


def shift_right(x, by):
    assert by & (by - 1) == 0
    return x >> (by.bit_length() - 1)


def place_sites(
    tile_rows, columns, reach, slots, reply_t, pix_refs, first_ref, second_ref, value_ref, place_ref, tall_ref, flat_ref
):
    halves = columns // LANES
    for t, (down, right) in enumerate(NEIGHBOURS):
        pix = pix_refs[right + 1][(down + 1) * slots : (down + 2) * slots, :]
        row, col = shift_right(pix, columns), pix & (columns - 1)
        row = row - (tile_rows - reach) if down < 0 else row
        height = reach if down else tile_rows
        block = pl.ds(t * slots, slots)
        if right:
            first_ref[block, :] = row
            second_ref[block, :] = col - (columns - reach) if right < 0 else col
        else:
            inside = (row >= 0) & (row < height)
            line = shift_right(col, LANES) * height + row
            first_ref[block, :] = jnp.where(inside, line, -1)
            second_ref[block, :] = col & (LANES - 1)

    def one(c, carry):
        value, where, tall, flat = [], [], [], []
        narrow, narrow_where = [], []
        for t, (down, right) in enumerate(NEIGHBOURS):
            reply = reply_t[pl.ds(t * slots + c, 1), :]
            first = first_ref[pl.ds(t * slots + c, 1), :]
            second = second_ref[pl.ds(t * slots + c, 1), :]
            height = reach if down else tile_rows
            if right:
                narrow.append(spread(reply, first, height))
                narrow_where.append(spread(1.0, second, reach))
                continue
            part = spread(reply, first, halves * height)
            (tall if down else value).append(part)
            (flat if down else where).append(spread(1.0, second, LANES))
        value_ref[c] = jnp.concatenate(value + narrow, axis=0)
        rest = jnp.zeros((place_ref.shape[1] - LANES - len(narrow_where) * reach, LANES), bf16)
        place_ref[c] = jnp.concatenate(where + narrow_where + [rest], axis=0)
        tall_ref[c] = jnp.concatenate(tall, axis=0)
        flat_ref[c] = jnp.concatenate(flat, axis=0)
        return carry

    lax.fori_loop(0, slots, one, 0, unroll=UNROLL["site"])


def finish_kernel(
    taps,
    slots,
    grid_rows,
    grid_cols,
    gain_ref,
    reply_ref,
    low_ref,
    pix_ref,
    high_ref,
    target_ref,
    inten_ref,
    fields_hbm,
    table_hbm,
    out_ref,
    fields_ref,
    table_ref,
    reply_t,
    first_ref,
    second_ref,
    value_ref,
    place_ref,
    tall_ref,
    flat_ref,
    weighted_ref,
    part_ref,
    sems,
):
    fields_copy = pltpu.make_async_copy(fields_hbm, fields_ref, sems.at[0])
    table_copy = pltpu.make_async_copy(table_hbm, table_ref, sems.at[1])
    fields_copy.start()
    table_copy.start()
    rows, columns = out_ref.shape
    height, width = inten_ref.shape
    reach = (height - rows) // 2
    halves = columns // LANES
    for block in range(reply_ref.shape[1]):
        reply_t[block * LANES : (block + 1) * LANES, :] = reply_ref[:, block, :].T
    pix_refs = (low_ref, pix_ref, high_ref)
    place_sites(
        rows, columns, reach, slots, reply_t, pix_refs, first_ref, second_ref, value_ref, place_ref, tall_ref, flat_ref
    )
    near_sum = product_nt(side_by_side(value_ref), side_by_side(place_ref))
    tall_sum = product_nt(side_by_side(tall_ref), side_by_side(flat_ref))

    def across(block, size):
        return jnp.concatenate(
            [block[half * size : (half + 1) * size] for half in range(halves)]
            + [jnp.zeros((size, width - columns), f32)],
            axis=1,
        )

    middle = near_sum[: halves * rows, :LANES]
    above = tall_sum[: halves * reach, :LANES]
    below = tall_sum[halves * reach :, LANES : 2 * LANES]
    scattered = jnp.concatenate(
        [across(above, reach), across(middle, rows), across(below, reach)], axis=0
    )
    scattered = pltpu.roll(scattered, reach, axis=1)
    start = halves * rows
    lane = lax.broadcasted_iota(jnp.int32, (height, LANES), 1)
    sides = []
    for side in range(2):
        strips = []
        for place in range(3):
            size = rows if place == 1 else reach
            strip = near_sum[start : start + size, LANES : 2 * LANES]
            shift = (side * reach - (side * 3 + place) * reach) % LANES
            strips.append(pltpu.roll(strip, shift, axis=1) if shift else strip)
            start += size
        strip = jnp.concatenate(strips, axis=0)
        here = (lane >= side * reach) & (lane < (side + 1) * reach)
        sides.append(jnp.where(here, strip, 0.0))
    gap = jnp.zeros((height, LANES), f32)
    strips = [sides[0]] + [gap] * (halves - 1) + [sides[1]]

    nominal = jax.nn.sigmoid(steepness * (inten_ref[...] - threshold))
    first = pix_ref.shape[0]
    target = jnp.concatenate([low_ref[first:, :], target_ref[...], high_ref[first:, :]], axis=1)
    target = pltpu.roll(target.astype(f32), target.shape[1] - (LANES - reach), axis=1)
    dense = (nominal - target[:, :width]) * steepness * nominal * (1.0 - nominal)
    slope = dense + scattered + jnp.concatenate(strips, axis=1)
    line = lax.broadcasted_iota(jnp.int32, (height, width), 0) - reach
    line = line + lax.axis_index("row") * rows
    column = lax.broadcasted_iota(jnp.int32, (height, width), 1) - reach
    inside = (column < columns + reach) & (line >= 0) & (line < grid_rows * rows)
    column = column + lax.axis_index("col") * columns
    inside = inside & (column >= 0) & (column < grid_cols * columns)
    slope = jnp.where(inside, slope, 0.0)

    def weigh(h, carry):
        start = pl.multiple_of(h * height, height)
        field = fields_ref[pl.ds(start, height), :]
        weighted_ref[pl.ds(start, height), :] = (gain_ref[h // 2] * field * slope).astype(bf16)
        return carry

    fields_copy.wait()
    lax.fori_loop(0, weighted_ref.shape[0] // height, weigh, 0, unroll=UNROLL["weigh"])
    table_copy.wait()
    part_ref[...] = jnp.dot(table_ref[...], weighted_ref[...], preferred_element_type=f32)

    def gather(v, total):
        start = pl.multiple_of(v * rows, rows)
        return total + pltpu.roll(part_ref[pl.ds(start, rows), :], width - v, axis=1)[:, :columns]

    total = jnp.zeros((rows, columns), f32)
    total = lax.fori_loop(0, taps, gather, total, unroll=UNROLL["gather"])
    out_ref[...] = 2.0 * total


def round_up(x, to):
    return -(-x // to) * to


def lines_of(taps, stride, length):
    count, blocks, extent = taps.shape
    padded = jnp.pad(taps, ((0, 0), (0, 0), (0, stride - extent)))
    flat = padded.reshape(count, blocks * stride)
    return jnp.pad(flat, ((0, 0), (0, length - blocks * stride))).astype(f32)


def body(mask, target, kernels, weights, doses, site_pix, send_count, recv_frag, frag_target):
    rows, columns = mask.shape
    extent = kernels.shape[-1]
    reach = extent // 2
    kernel_taps = kernels.reshape(-1, extent, extent)
    parts = kernel_taps.shape[0]
    owners, slots = site_pix.shape
    conds = doses.shape[0]
    both = ("row", "col")

    wide = 2 * reach
    pix = site_pix.T
    low, high = clipped(*ring(mask[:wide], mask[rows - wide :], "row"), "row")
    near = jnp.concatenate([low, mask, high], axis=0)
    near, pix, target = lax.optimization_barrier((near, pix, target))
    low, high = clipped(*ring(near[:, :wide], near[:, columns - wide :], "col"), "col")
    near = jnp.concatenate([low, near, high], axis=1)
    wide_columns = round_up(near.shape[1], LANES)
    near = jnp.pad(near, ((0, 0), (0, wide_columns - near.shape[1])))

    halves = columns // LANES

    def pixels_and(aim):
        lanes = [aim[:, half * LANES : (half + 1) * LANES] for half in range(halves)]
        return jnp.concatenate([pix] + lanes, axis=0)

    low, high = ring(pixels_and(target[:reach]), pixels_and(target[rows - reach :]), "row")
    pix_column = jnp.concatenate([low[:slots], pix, high[:slots]], axis=0)
    target_column = jnp.concatenate(
        [
            jnp.concatenate(
                [side[slots + half * reach :][:reach] for half in range(halves)], axis=1
            )
            if side is not None
            else target
            for side in (low, None, high)
        ],
        axis=0,
    )

    height = rows + 2 * reach
    by_column = kernel_taps.transpose(0, 2, 1)
    core_depth = round_up(extent * height, LANES)
    core_table = banded(lines_of(by_column, height, core_depth), rows)

    level = call(
        functools.partial(forward_kernel, extent, reach),
        jax.ShapeDtypeStruct((owners, LANES), f32),
        scratch=[
            pltpu.VMEM((core_depth, columns), bf16),
            pltpu.VMEM((rows * columns // LANES, LANES), f32),
        ],
        inputs=5,
        smem=(0,),
        flops=2 * parts * rows * core_depth * columns,
        moved=2 * parts * rows * core_depth,
    )(weights, near, core_table, pix, send_count)

    flipped = kernel_taps[:, ::-1, ::-1].transpose(2, 0, 1)
    back_depth = parts * height
    back_lines = lines_of(flipped, height, back_depth)
    level, pix_column, target_column, back_lines = lax.optimization_barrier(
        (level, pix_column, target_column, back_lines)
    )
    arrived = lax.all_to_all(level, both, split_axis=0, concat_axis=0, tiled=True)
    back_table = banded(back_lines, rows)
    arrived, back_table = lax.optimization_barrier((arrived, back_table))
    low, high = ring(
        jnp.concatenate([pix_column, target_column[:, :LANES]], axis=0),
        jnp.concatenate([pix_column, target_column[:, columns - LANES :]], axis=0),
        "col",
    )
    grid_rows, grid_cols = lax.axis_size("row"), lax.axis_size("col")
    blocks = round_up(len(NEIGHBOURS) * slots, LANES) // LANES
    frag_error, answers = call(
        functools.partial(owner_kernel, grid_rows, grid_cols),
        (
            jax.ShapeDtypeStruct(frag_target.shape, f32),
            jax.ShapeDtypeStruct((owners, blocks, LANES), f32),
        ),
        scratch=[
            pltpu.VMEM((LANES, LANES), f32),
            pltpu.VMEM((slots, LANES), f32),
            pltpu.VMEM((slots, conds, LANES), f32),
            pltpu.VMEM((slots, frag_target.size // LANES, LANES), bf16),
            pltpu.VMEM((slots, LANES, LANES), bf16),
            pltpu.VMEM((blocks * LANES, LANES), f32),
        ],
        inputs=4,
        flops=2 * 2 * frag_target.size * site_pix.size // 16,
        moved=8 * frag_target.size,
    )(doses[:, None], arrived, recv_frag.T, frag_target)

    tall = rows + 4 * reach
    wide_depth = round_up(extent * tall, LANES)
    wide_lines = lines_of(by_column, tall, wide_depth)
    answers, near, wide_lines = lax.optimization_barrier((answers, near, wide_lines))
    returned = lax.all_to_all(answers, both, split_axis=0, concat_axis=0, tiled=True)
    wide_fields, wide_intensity = call(
        functools.partial(wide_kernel, extent, height, parts * height // 2),
        (
            pltpu.HBM((parts * height, wide_columns), f32),
            jax.ShapeDtypeStruct((height, wide_columns), f32),
        ),
        scratch=[
            pltpu.VMEM((parts * height, wide_columns), f32),
            pltpu.VMEM((parts * height, wide_depth), bf16),
            pltpu.VMEM((wide_depth, wide_columns), bf16),
            pltpu.SemaphoreType.DMA((2,)),
        ],
        inputs=3,
        smem=(0,),
        hbm_out=(0,),
        vmem_mib=24,
        flops=2 * parts * height * wide_depth * wide_columns,
        moved=4 * parts * height * wide_columns,
    )(weights, near, wide_lines)
    returned, wide_fields, wide_intensity, low, high = lax.optimization_barrier(
        (returned, wide_fields, wide_intensity, low, high)
    )
    wide_fields = pltpu.with_memory_space_constraint(wide_fields, pltpu.HBM)
    back_table = pltpu.with_memory_space_constraint(back_table, pltpu.HBM)
    gradient = call(
        functools.partial(finish_kernel, extent, slots, grid_rows, grid_cols),
        jax.ShapeDtypeStruct((rows, columns), f32),
        scratch=[
            pltpu.VMEM(wide_fields.shape, f32),
            pltpu.VMEM(back_table.shape, bf16),
            pltpu.VMEM((blocks * LANES, LANES), f32),
            pltpu.VMEM((blocks * LANES, LANES), jnp.int32),
            pltpu.VMEM((blocks * LANES, LANES), jnp.int32),
            pltpu.VMEM((slots, halves * rows + 2 * (rows + 2 * reach), LANES), bf16),
            pltpu.VMEM((slots, 2 * LANES, LANES), bf16),
            pltpu.VMEM((slots, 2 * halves * reach, LANES), bf16),
            pltpu.VMEM((slots, 2 * LANES, LANES), bf16),
            pltpu.VMEM((back_depth, wide_columns), bf16),
            pltpu.VMEM((extent * rows, wide_columns), f32),
            pltpu.SemaphoreType.DMA((2,)),
        ],
        inputs=9,
        smem=(0,),
        hbm=(7, 8),
        vmem_mib=32,
        flops=2 * extent * rows * back_depth * wide_columns,
        moved=8 * back_depth * wide_columns,
    )(
        weights,
        returned,
        low,
        pix_column,
        high,
        target_column,
        wide_intensity,
        wide_fields,
        back_table,
    )
    return gradient, frag_error


def solution(mesh):
    return jax.shard_map(
        body,
        mesh=mesh,
        in_specs=(
            P("row", "col"),
            P("row", "col"),
            P(),
            P(),
            P(),
            P("row", "col"),
            P("row", "col"),
            P("row", "col"),
            P(None, ("row", "col")),
        ),
        out_specs=(P("row", "col"), P(None, ("row", "col"))),
        check_vma=False,
    )
```

```python
import functools

import jax
import jax.numpy as jnp
from jax import lax
from jax.experimental import pallas as pl
from jax.experimental.pallas import tpu as pltpu
from jax.sharding import PartitionSpec as P

steepness = 4.0
threshold = 1.2
f32 = jnp.float32
bf16 = jnp.bfloat16
LANES = 128
NEIGHBOURS = [(down, right) for right in (-1, 0, 1) for down in (-1, 0, 1)]
MIB = 1 << 20
UNROLL = {
    "table": 4,
    "stack": 33,
    "wide": 3,
    "pick": 32,
    "owner": 4,
    "answer": 16,
    "site": 4,
    "weigh": 16,
    "gather": 33,
}


def call(
    kernel, out_shapes, scratch=(), flops=0, moved=0, smem=(), hbm=(), hbm_out=(), inputs=0, vmem_mib=16
):
    vmem = pl.BlockSpec(memory_space=pltpu.VMEM)
    specs = [vmem] * inputs
    for i in smem:
        specs[i] = pl.BlockSpec(memory_space=pltpu.SMEM)
    for i in hbm:
        specs[i] = pl.BlockSpec(memory_space=pltpu.HBM)
    out_specs = jax.tree.map(lambda _: vmem, out_shapes)
    if hbm_out:
        out_specs = tuple(
            pl.BlockSpec(memory_space=pltpu.HBM) if i in hbm_out else vmem
            for i in range(len(out_shapes))
        )
    return pl.pallas_call(
        kernel,
        out_shape=out_shapes,
        in_specs=specs,
        out_specs=out_specs,
        scratch_shapes=list(scratch),
        cost_estimate=pl.CostEstimate(flops=flops, bytes_accessed=moved, transcendentals=0),
        compiler_params=pltpu.CompilerParams(vmem_limit_bytes=vmem_mib * MIB),
    )


def ring(low_end, high_end, axis):
    count = lax.axis_size(axis)
    up = [(i, (i + 1) % count) for i in range(count)]
    down = [(target, source) for source, target in up]
    return lax.ppermute(high_end, axis, up), lax.ppermute(low_end, axis, down)


def clipped(low, high, axis):
    index = lax.axis_index(axis)
    zero = jnp.zeros((), low.dtype)
    low = jnp.where(index == 0, zero, low)
    return low, jnp.where(index == lax.axis_size(axis) - 1, zero, high)


def shear(row, rows):
    wide = jnp.broadcast_to(row, (rows, row.shape[1]))
    return pltpu.roll(wide, 0, axis=1, stride=1, stride_axis=0)


def fill_table(rows, first, last, lines_ref, table_ref):
    def one(index, carry):
        line = lines_ref[pl.ds(index, 1), :]
        start = pl.multiple_of(index * rows, rows)
        table_ref[pl.ds(start, rows), :] = shear(line, rows).astype(bf16)
        return carry

    lax.fori_loop(first, last, one, 0, unroll=UNROLL["table"])


def table_kernel(rows, lines_ref, out_ref):
    fill_table(rows, 0, lines_ref.shape[0], lines_ref, out_ref)


def back_table_kernel(rows, lines_ref, out_hbm, out_ref, sem):
    fill_table(rows, 0, lines_ref.shape[0], lines_ref, out_ref)
    copy = pltpu.make_async_copy(out_ref, out_hbm, sem.at[0])
    copy.start()
    copy.wait()


def stack_shifts(plane, taps, first, out_ref):
    height, width = plane.shape
    columns = out_ref.shape[1]

    def one(v, carry):
        moved = pltpu.roll(plane, width - first - v, axis=1)[:, :columns]
        start = pl.multiple_of(v * height, height)
        out_ref[pl.ds(start, height), :] = moved.astype(bf16)
        return carry

    lax.fori_loop(0, taps, one, 0, unroll=UNROLL["stack"])
    rest = out_ref.shape[0] - taps * height
    out_ref[taps * height :, :] = jnp.zeros((rest, columns), bf16)


def forward_kernel(
    taps,
    reach,
    gain_ref,
    mask_ref,
    table_ref,
    pix_ref,
    count_ref,
    level_ref,
    table_hbm,
    stack_ref,
    lines_ref,
    sem,
):
    columns = stack_ref.shape[1]
    halves = columns // LANES
    rows = lines_ref.shape[0] // halves
    store = pltpu.make_async_copy(table_ref, table_hbm, sem.at[0])
    store.start()
    plane = mask_ref[reach : reach + rows + 2 * reach, :].astype(f32)
    stack_shifts(plane, taps, reach, stack_ref)
    fields = jnp.dot(table_ref[...], stack_ref[...], preferred_element_type=f32)
    total = jnp.zeros((rows, columns), f32)
    for k in range(gain_ref.shape[0]):
        real = fields[2 * k * rows : (2 * k + 1) * rows]
        imag = fields[(2 * k + 1) * rows : (2 * k + 2) * rows]
        total = total + gain_ref[k] * (real * real + imag * imag)
    for half in range(halves):
        lines_ref[half * rows : (half + 1) * rows, :] = total[:, half * LANES : (half + 1) * LANES]
    pix = pix_ref[...]
    slots, owners = pix.shape
    low = pix & (LANES - 1)
    high = pix >> 7

    def pick(i, level):
        for half in range(halves):
            line = lines_ref[pl.ds(half * rows + i, 1), :]
            wide = jnp.broadcast_to(line, (slots, LANES))
            found = jnp.take_along_axis(wide, low, axis=1, mode="promise_in_bounds")
            level = jnp.where(high == i * halves + half, found, level)
        return level

    level = lax.fori_loop(0, rows, pick, jnp.zeros((slots, owners), f32), unroll=UNROLL["pick"])
    live = lax.broadcasted_iota(jnp.int32, (slots, owners), 0) < count_ref[...]
    level = jnp.where(live, level, -1.0)
    level = jnp.concatenate([level, jnp.zeros((owners - slots, owners), f32)], axis=0)
    level_ref[...] = level.T
    store.wait()


def stack_wide_shifts(plane, taps, columns, extra, stack_ref):
    width = plane.shape[1]
    height = stack_ref.shape[0] // taps // 8 * 8
    lane = lax.broadcasted_iota(jnp.int32, (height, width - columns), 1)

    def one(v, carry):
        moved = pltpu.roll(plane, width - v, axis=1)
        first, second = moved[:height], moved[plane.shape[0] - height :]
        rest = pltpu.roll(second[:, columns:], extra, axis=1)
        rest = jnp.where(lane < extra, first[:, columns:], rest)
        start = pl.multiple_of(v * height, height)
        stack_ref[pl.ds(start, height), :columns] = first[:, :columns].astype(bf16)
        stack_ref[pl.ds(start, height), columns : 2 * columns] = second[:, :columns].astype(bf16)
        stack_ref[pl.ds(start, height), 2 * columns :] = rest.astype(bf16)
        return carry

    lax.fori_loop(0, taps, one, 0, unroll=UNROLL["wide"])
    rest = stack_ref.shape[0] - taps * height
    stack_ref[taps * height :, :] = jnp.zeros((rest, stack_ref.shape[1]), bf16)


def wide_kernel(
    taps,
    columns,
    extra,
    gain_ref,
    near_ref,
    table_hbm,
    fields_hbm,
    inten_ref,
    fields_ref,
    table_ref,
    stack_ref,
    in_sem,
    out_sems,
):
    load = pltpu.make_async_copy(table_hbm, table_ref, in_sem.at[0])
    load.start()
    stack_wide_shifts(near_ref[...].astype(f32), taps, columns, extra, stack_ref)
    load.wait()
    fields = jnp.dot(table_ref[...], stack_ref[...], preferred_element_type=f32)
    size = fields.shape[0]
    lanes = fields.shape[1] - 2 * columns
    rows = inten_ref.shape[0] // 2
    stores = []
    for half in range(2):
        ends = fields[:, 2 * columns :]
        if half:
            ends = pltpu.roll(ends, lanes - extra, axis=1)
        part = pl.ds(half * size, size)
        fields_ref[part, :columns] = fields[:, half * columns : (half + 1) * columns]
        fields_ref[part, columns:] = ends
        stores.append(
            pltpu.make_async_copy(fields_ref.at[part], fields_hbm.at[part], out_sems.at[half])
        )
        stores[-1].start()
    for half in range(2):
        total = jnp.zeros((rows, inten_ref.shape[1]), f32)
        for k in range(gain_ref.shape[0]):
            start = half * size + 2 * k * rows
            real = fields_ref[start : start + rows, :]
            imag = fields_ref[start + rows : start + 2 * rows, :]
            total = total + gain_ref[k] * (real * real + imag * imag)
        inten_ref[half * rows : (half + 1) * rows, :] = total
    for store in stores:
        store.wait()


def spread(value, index, size):
    here = lax.broadcasted_iota(jnp.int32, (size, LANES), 0) == index
    return jnp.where(here, value, 0.0).astype(bf16)


def product_nt(a, b):
    return lax.dot_general(a, b, (((1,), (1,)), ((), ())), preferred_element_type=f32)


def side_by_side(ref):
    return jnp.concatenate([ref[c] for c in range(ref.shape[0])], axis=1)


def owner_kernel(
    grid_rows,
    grid_cols,
    dose_ref,
    level_ref,
    frag_ref,
    aim_ref,
    error_ref,
    slope_ref,
    level_t,
    slope_t,
    resist_ref,
    value_ref,
    place_ref,
    around_t,
):
    slots = frag_ref.shape[0]
    conds = dose_ref.shape[0]
    bins = aim_ref.shape[1] // LANES
    level_t[...] = level_ref[...].T
    dose = jnp.broadcast_to(dose_ref[...], (conds, LANES))

    def place(c, carry):
        level = jnp.broadcast_to(level_t[pl.ds(c, 1), :], (conds, LANES))
        resist = jax.nn.sigmoid(steepness * (dose * level - threshold))
        live = level >= 0.0
        resist_ref[c] = jnp.where(live, resist, 0.0)
        frag = frag_ref[pl.ds(c, 1), :]
        bin_of = jnp.broadcast_to(frag >> 7, (conds, LANES))
        value_ref[c] = jnp.concatenate(
            [jnp.where(bin_of == q, resist_ref[c], 0.0) for q in range(bins)], axis=0
        ).astype(bf16)
        place_ref[c] = spread(1.0, frag & (LANES - 1), LANES)
        return carry

    lax.fori_loop(0, slots, place, 0, unroll=UNROLL["owner"])
    total = product_nt(side_by_side(value_ref), side_by_side(place_ref))
    for q in range(bins):
        lanes = slice(q * LANES, (q + 1) * LANES)
        error_ref[:, lanes] = total[q * conds : (q + 1) * conds] - aim_ref[:, lanes]

    def answer(c, carry):
        resist = resist_ref[c]
        frag = jnp.broadcast_to(frag_ref[pl.ds(c, 1), :], (conds, LANES))
        low = frag & (LANES - 1)
        bin_of = frag >> 7
        reply = jnp.zeros((conds, LANES), f32)
        for q in range(bins):
            found = jnp.take_along_axis(
                error_ref[:, q * LANES : (q + 1) * LANES], low, axis=1, mode="promise_in_bounds"
            )
            reply = jnp.where(bin_of == q, found, reply)
        terms = reply * steepness * dose * resist * (1.0 - resist)
        slope_t[pl.ds(c, 1), :] = jnp.sum(terms, axis=0, keepdims=True)
        return carry

    lax.fori_loop(0, slots, answer, 0, unroll=UNROLL["answer"])
    slope = slope_t[:slots, :]
    lane = lax.broadcasted_iota(jnp.int32, (slots, LANES), 1)
    tile_row, tile_col = lane // grid_cols, lane % grid_cols
    for t, (down, right) in enumerate(NEIGHBOURS):
        row, col = tile_row + down, tile_col + right
        inside = (row >= 0) & (row < grid_rows) & (col >= 0) & (col < grid_cols)
        moved = pltpu.roll(slope, -(down * grid_cols + right) % LANES, axis=1)
        around_t[t * slots : (t + 1) * slots, :] = jnp.where(inside, moved, 0.0)
    rest = around_t.shape[0] - len(NEIGHBOURS) * slots
    around_t[len(NEIGHBOURS) * slots :, :] = jnp.zeros((rest, LANES), f32)
    for block in range(around_t.shape[0] // LANES):
        slope_ref[:, block, :] = around_t[block * LANES : (block + 1) * LANES, :].T


def shift_right(x, by):
    assert by & (by - 1) == 0
    return x >> (by.bit_length() - 1)


def place_sites(
    tile_rows, columns, reach, slots, reply_t, pix_refs, first_ref, second_ref, value_ref, place_ref, tall_ref, flat_ref
):
    halves = columns // LANES
    for t, (down, right) in enumerate(NEIGHBOURS):
        pix = pix_refs[right + 1][(down + 1) * slots : (down + 2) * slots, :]
        row, col = shift_right(pix, columns), pix & (columns - 1)
        row = row - (tile_rows - reach) if down < 0 else row
        height = reach if down else tile_rows
        block = pl.ds(t * slots, slots)
        if right:
            first_ref[block, :] = row
            second_ref[block, :] = col - (columns - reach) if right < 0 else col
        else:
            inside = (row >= 0) & (row < height)
            line = shift_right(col, LANES) * height + row
            first_ref[block, :] = jnp.where(inside, line, -1)
            second_ref[block, :] = col & (LANES - 1)

    def one(c, carry):
        value, where, tall, flat = [], [], [], []
        narrow, narrow_where = [], []
        for t, (down, right) in enumerate(NEIGHBOURS):
            reply = reply_t[pl.ds(t * slots + c, 1), :]
            first = first_ref[pl.ds(t * slots + c, 1), :]
            second = second_ref[pl.ds(t * slots + c, 1), :]
            height = reach if down else tile_rows
            if right:
                narrow.append(spread(reply, first, height))
                narrow_where.append(spread(1.0, second, reach))
                continue
            part = spread(reply, first, halves * height)
            (tall if down else value).append(part)
            (flat if down else where).append(spread(1.0, second, LANES))
        value_ref[c] = jnp.concatenate(value + narrow, axis=0)
        rest = jnp.zeros((place_ref.shape[1] - LANES - len(narrow_where) * reach, LANES), bf16)
        place_ref[c] = jnp.concatenate(where + narrow_where + [rest], axis=0)
        tall_ref[c] = jnp.concatenate(tall, axis=0)
        flat_ref[c] = jnp.concatenate(flat, axis=0)
        return carry

    lax.fori_loop(0, slots, one, 0, unroll=UNROLL["site"])


def finish_kernel(
    taps,
    slots,
    grid_rows,
    grid_cols,
    gain_ref,
    reply_ref,
    low_ref,
    pix_ref,
    high_ref,
    target_ref,
    inten_ref,
    fields_hbm,
    table_hbm,
    out_ref,
    fields_ref,
    table_ref,
    reply_t,
    first_ref,
    second_ref,
    value_ref,
    place_ref,
    tall_ref,
    flat_ref,
    weighted_ref,
    part_ref,
    sems,
):
    fields_copy = pltpu.make_async_copy(fields_hbm, fields_ref, sems.at[0])
    table_copy = pltpu.make_async_copy(table_hbm, table_ref, sems.at[1])
    fields_copy.start()
    table_copy.start()
    rows, columns = out_ref.shape
    height, width = inten_ref.shape
    reach = (height - rows) // 2
    halves = columns // LANES
    for block in range(reply_ref.shape[1]):
        reply_t[block * LANES : (block + 1) * LANES, :] = reply_ref[:, block, :].T
    pix_refs = (low_ref, pix_ref, high_ref)
    place_sites(
        rows, columns, reach, slots, reply_t, pix_refs, first_ref, second_ref, value_ref, place_ref, tall_ref, flat_ref
    )
    near_sum = product_nt(side_by_side(value_ref), side_by_side(place_ref))
    tall_sum = product_nt(side_by_side(tall_ref), side_by_side(flat_ref))

    def across(block, size):
        return jnp.concatenate(
            [block[half * size : (half + 1) * size] for half in range(halves)]
            + [jnp.zeros((size, width - columns), f32)],
            axis=1,
        )

    middle = near_sum[: halves * rows, :LANES]
    above = tall_sum[: halves * reach, :LANES]
    below = tall_sum[halves * reach :, LANES : 2 * LANES]
    scattered = jnp.concatenate(
        [across(above, reach), across(middle, rows), across(below, reach)], axis=0
    )
    scattered = pltpu.roll(scattered, reach, axis=1)
    start = halves * rows
    lane = lax.broadcasted_iota(jnp.int32, (height, LANES), 1)
    sides = []
    for side in range(2):
        strips = []
        for place in range(3):
            size = rows if place == 1 else reach
            strip = near_sum[start : start + size, LANES : 2 * LANES]
            shift = (side * reach - (side * 3 + place) * reach) % LANES
            strips.append(pltpu.roll(strip, shift, axis=1) if shift else strip)
            start += size
        strip = jnp.concatenate(strips, axis=0)
        here = (lane >= side * reach) & (lane < (side + 1) * reach)
        sides.append(jnp.where(here, strip, 0.0))
    gap = jnp.zeros((height, LANES), f32)
    strips = [sides[0]] + [gap] * (halves - 1) + [sides[1]]

    nominal = jax.nn.sigmoid(steepness * (inten_ref[...] - threshold))
    first = pix_ref.shape[0]
    target = jnp.concatenate([low_ref[first:, :], target_ref[...], high_ref[first:, :]], axis=1)
    target = pltpu.roll(target.astype(f32), target.shape[1] - (LANES - reach), axis=1)
    dense = (nominal - target[:, :width]) * steepness * nominal * (1.0 - nominal)
    slope = dense + scattered + jnp.concatenate(strips, axis=1)
    line = lax.broadcasted_iota(jnp.int32, (height, width), 0) - reach
    line = line + lax.axis_index("row") * rows
    column = lax.broadcasted_iota(jnp.int32, (height, width), 1) - reach
    inside = (column < columns + reach) & (line >= 0) & (line < grid_rows * rows)
    column = column + lax.axis_index("col") * columns
    inside = inside & (column >= 0) & (column < grid_cols * columns)
    slope = jnp.where(inside, slope, 0.0)

    upper = height // 2
    parts = weighted_ref.shape[0] // height

    def weigh(h, carry):
        for half in range(2):
            lines = pl.ds(pl.multiple_of((half * parts + h) * upper, upper), upper)
            weight = gain_ref[h // 2] * fields_ref[lines, :]
            lines = pl.ds(pl.multiple_of(h * height + half * upper, upper), upper)
            weighted = weight * slope[half * upper : (half + 1) * upper]
            weighted_ref[lines, :] = weighted.astype(bf16)
        return carry

    fields_copy.wait()
    lax.fori_loop(0, weighted_ref.shape[0] // height, weigh, 0, unroll=UNROLL["weigh"])
    table_copy.wait()
    part_ref[...] = jnp.dot(table_ref[...], weighted_ref[...], preferred_element_type=f32)

    def gather(v, total):
        start = pl.multiple_of(v * rows, rows)
        return total + pltpu.roll(part_ref[pl.ds(start, rows), :], width - v, axis=1)[:, :columns]

    total = jnp.zeros((rows, columns), f32)
    total = lax.fori_loop(0, taps, gather, total, unroll=UNROLL["gather"])
    out_ref[...] = 2.0 * total


def round_up(x, to):
    return -(-x // to) * to


def lines_of(taps, stride, length):
    count, blocks, extent = taps.shape
    padded = jnp.pad(taps, ((0, 0), (0, 0), (0, stride - extent)))
    flat = padded.reshape(count, blocks * stride)
    return jnp.pad(flat, ((0, 0), (0, length - blocks * stride))).astype(f32)


def body(mask, target, kernels, weights, doses, site_pix, send_count, recv_frag, frag_target):
    rows, columns = mask.shape
    extent = kernels.shape[-1]
    reach = extent // 2
    kernel_taps = kernels.reshape(-1, extent, extent)
    parts = kernel_taps.shape[0]
    owners, slots = site_pix.shape
    conds = doses.shape[0]
    both = ("row", "col")

    wide = 2 * reach
    pix = site_pix.T
    low, high = clipped(*ring(mask[:wide], mask[rows - wide :], "row"), "row")
    near = jnp.concatenate([low, mask, high], axis=0)
    near, pix, target = lax.optimization_barrier((near, pix, target))
    low, high = clipped(*ring(near[:, :wide], near[:, columns - wide :], "col"), "col")
    near = jnp.concatenate([low, near, high], axis=1)
    wide_columns = round_up(near.shape[1], LANES)
    near = jnp.pad(near, ((0, 0), (0, wide_columns - near.shape[1])))

    halves = columns // LANES

    def pixels_and(aim):
        lanes = [aim[:, half * LANES : (half + 1) * LANES] for half in range(halves)]
        return jnp.concatenate([pix] + lanes, axis=0)

    low, high = ring(pixels_and(target[:reach]), pixels_and(target[rows - reach :]), "row")
    pix_column = jnp.concatenate([low[:slots], pix, high[:slots]], axis=0)
    target_column = jnp.concatenate(
        [
            jnp.concatenate(
                [side[slots + half * reach :][:reach] for half in range(halves)], axis=1
            )
            if side is not None
            else target
            for side in (low, None, high)
        ],
        axis=0,
    )

    height = rows + 2 * reach
    by_column = kernel_taps.transpose(0, 2, 1)
    core_depth = round_up(extent * height, LANES)
    core_shape = (parts * rows, core_depth)
    core_table = call(
        functools.partial(table_kernel, rows),
        jax.ShapeDtypeStruct(core_shape, bf16),
        inputs=1,
        moved=2 * parts * rows * core_depth,
    )(lines_of(by_column, height, core_depth))

    level, stored_table = call(
        functools.partial(forward_kernel, extent, reach),
        (jax.ShapeDtypeStruct((owners, LANES), f32), pltpu.HBM(core_shape, bf16)),
        scratch=[
            pltpu.VMEM((core_depth, columns), bf16),
            pltpu.VMEM((rows * columns // LANES, LANES), f32),
            pltpu.SemaphoreType.DMA((1,)),
        ],
        inputs=5,
        smem=(0,),
        hbm_out=(1,),
        flops=2 * parts * rows * core_depth * columns,
        moved=2 * parts * rows * core_depth,
    )(weights, near, core_table, pix, send_count)

    flipped = kernel_taps[:, ::-1, ::-1].transpose(2, 0, 1)
    back_depth = parts * height
    level, pix_column, target_column, back_lines = lax.optimization_barrier(
        (level, pix_column, target_column, lines_of(flipped, height, back_depth))
    )
    arrived = lax.all_to_all(level, both, split_axis=0, concat_axis=0, tiled=True)
    back_shape = (extent * rows, back_depth)
    (back_table,) = call(
        functools.partial(back_table_kernel, rows),
        (pltpu.HBM(back_shape, bf16),),
        scratch=[pltpu.VMEM(back_shape, bf16), pltpu.SemaphoreType.DMA((1,))],
        inputs=1,
        hbm_out=(0,),
        moved=2 * extent * rows * back_depth,
    )(back_lines)
    arrived, back_table = lax.optimization_barrier((arrived, back_table))
    low, high = ring(
        jnp.concatenate([pix_column, target_column[:, :LANES]], axis=0),
        jnp.concatenate([pix_column, target_column[:, columns - LANES :]], axis=0),
        "col",
    )
    grid_rows, grid_cols = lax.axis_size("row"), lax.axis_size("col")
    blocks = round_up(len(NEIGHBOURS) * slots, LANES) // LANES
    frag_error, answers = call(
        functools.partial(owner_kernel, grid_rows, grid_cols),
        (
            jax.ShapeDtypeStruct(frag_target.shape, f32),
            jax.ShapeDtypeStruct((owners, blocks, LANES), f32),
        ),
        scratch=[
            pltpu.VMEM((LANES, LANES), f32),
            pltpu.VMEM((slots, LANES), f32),
            pltpu.VMEM((slots, conds, LANES), f32),
            pltpu.VMEM((slots, frag_target.size // LANES, LANES), bf16),
            pltpu.VMEM((slots, LANES, LANES), bf16),
            pltpu.VMEM((blocks * LANES, LANES), f32),
        ],
        inputs=4,
        flops=2 * 2 * frag_target.size * site_pix.size // 16,
        moved=8 * frag_target.size,
    )(doses[:, None], arrived, recv_frag.T, frag_target)

    answers, near = lax.optimization_barrier((answers, near))
    returned = lax.all_to_all(answers, both, split_axis=0, concat_axis=0, tiled=True)
    wide_fields, wide_intensity = call(
        functools.partial(wide_kernel, extent, columns, wide),
        (
            pltpu.HBM((parts * height, wide_columns), f32),
            jax.ShapeDtypeStruct((height, wide_columns), f32),
        ),
        scratch=[
            pltpu.VMEM((parts * height, wide_columns), f32),
            pltpu.VMEM(core_shape, bf16),
            pltpu.VMEM((core_depth, columns + wide_columns), bf16),
            pltpu.SemaphoreType.DMA((1,)),
            pltpu.SemaphoreType.DMA((2,)),
        ],
        inputs=3,
        smem=(0,),
        hbm=(2,),
        hbm_out=(0,),
        vmem_mib=24,
        flops=2 * parts * rows * core_depth * (columns + wide_columns),
        moved=4 * parts * height * wide_columns,
    )(weights, near, pltpu.with_memory_space_constraint(stored_table, pltpu.HBM))
    returned, wide_fields, wide_intensity, low, high = lax.optimization_barrier(
        (returned, wide_fields, wide_intensity, low, high)
    )
    wide_fields = pltpu.with_memory_space_constraint(wide_fields, pltpu.HBM)
    back_table = pltpu.with_memory_space_constraint(back_table, pltpu.HBM)
    gradient = call(
        functools.partial(finish_kernel, extent, slots, grid_rows, grid_cols),
        jax.ShapeDtypeStruct((rows, columns), f32),
        scratch=[
            pltpu.VMEM(wide_fields.shape, f32),
            pltpu.VMEM(back_table.shape, bf16),
            pltpu.VMEM((blocks * LANES, LANES), f32),
            pltpu.VMEM((blocks * LANES, LANES), jnp.int32),
            pltpu.VMEM((blocks * LANES, LANES), jnp.int32),
            pltpu.VMEM((slots, halves * rows + 2 * (rows + 2 * reach), LANES), bf16),
            pltpu.VMEM((slots, 2 * LANES, LANES), bf16),
            pltpu.VMEM((slots, 2 * halves * reach, LANES), bf16),
            pltpu.VMEM((slots, 2 * LANES, LANES), bf16),
            pltpu.VMEM((back_depth, wide_columns), bf16),
            pltpu.VMEM((extent * rows, wide_columns), f32),
            pltpu.SemaphoreType.DMA((2,)),
        ],
        inputs=9,
        smem=(0,),
        hbm=(7, 8),
        vmem_mib=32,
        flops=2 * extent * rows * back_depth * wide_columns,
        moved=8 * back_depth * wide_columns,
    )(
        weights,
        returned,
        low,
        pix_column,
        high,
        target_column,
        wide_intensity,
        wide_fields,
        back_table,
    )
    return gradient, frag_error


def solution(mesh):
    return jax.shard_map(
        body,
        mesh=mesh,
        in_specs=(
            P("row", "col"),
            P("row", "col"),
            P(),
            P(),
            P(),
            P("row", "col"),
            P("row", "col"),
            P("row", "col"),
            P(None, ("row", "col")),
        ),
        out_specs=(P("row", "col"), P(None, ("row", "col"))),
        check_vma=False,
    )
```

```python
import functools

import jax
import jax.numpy as jnp
from jax import lax
from jax.experimental import pallas as pl
from jax.experimental.pallas import tpu as pltpu
from jax.sharding import PartitionSpec as P

steepness = 4.0
threshold = 1.2
f32 = jnp.float32
bf16 = jnp.bfloat16
LANES = 128
NEIGHBOURS = [(down, right) for right in (-1, 0, 1) for down in (-1, 0, 1)]
MIB = 1 << 20
UNROLL = {
    "table": 4,
    "stack": 33,
    "wide": 3,
    "pick": 32,
    "owner": 48,
    "answer": 24,
    "site": 4,
    "weigh": 16,
    "gather": 33,
}


def call(
    kernel, out_shapes, scratch=(), flops=0, moved=0, smem=(), hbm=(), hbm_out=(), inputs=0, vmem_mib=16
):
    vmem = pl.BlockSpec(memory_space=pltpu.VMEM)
    specs = [vmem] * inputs
    for i in smem:
        specs[i] = pl.BlockSpec(memory_space=pltpu.SMEM)
    for i in hbm:
        specs[i] = pl.BlockSpec(memory_space=pltpu.HBM)
    out_specs = jax.tree.map(lambda _: vmem, out_shapes)
    if hbm_out:
        out_specs = tuple(
            pl.BlockSpec(memory_space=pltpu.HBM) if i in hbm_out else vmem
            for i in range(len(out_shapes))
        )
    return pl.pallas_call(
        kernel,
        out_shape=out_shapes,
        in_specs=specs,
        out_specs=out_specs,
        scratch_shapes=list(scratch),
        cost_estimate=pl.CostEstimate(flops=flops, bytes_accessed=moved, transcendentals=0),
        compiler_params=pltpu.CompilerParams(vmem_limit_bytes=vmem_mib * MIB),
    )


def ring(low_end, high_end, axis):
    count = lax.axis_size(axis)
    up = [(i, (i + 1) % count) for i in range(count)]
    down = [(target, source) for source, target in up]
    return lax.ppermute(high_end, axis, up), lax.ppermute(low_end, axis, down)


def clipped(low, high, axis):
    index = lax.axis_index(axis)
    zero = jnp.zeros((), low.dtype)
    low = jnp.where(index == 0, zero, low)
    return low, jnp.where(index == lax.axis_size(axis) - 1, zero, high)


def shear(row, rows):
    wide = jnp.broadcast_to(row, (rows, row.shape[1]))
    return pltpu.roll(wide, 0, axis=1, stride=1, stride_axis=0)


def fill_table(rows, first, last, lines_ref, table_ref):
    def one(index, carry):
        line = lines_ref[pl.ds(index, 1), :]
        start = pl.multiple_of(index * rows, rows)
        table_ref[pl.ds(start, rows), :] = shear(line, rows).astype(bf16)
        return carry

    lax.fori_loop(first, last, one, 0, unroll=UNROLL["table"])


def table_kernel(rows, lines_ref, out_ref):
    fill_table(rows, 0, lines_ref.shape[0], lines_ref, out_ref)


def back_table_kernel(rows, lines_ref, out_hbm, out_ref, sem):
    fill_table(rows, 0, lines_ref.shape[0], lines_ref, out_ref)
    copy = pltpu.make_async_copy(out_ref, out_hbm, sem.at[0])
    copy.start()
    copy.wait()


def stack_shifts(plane, taps, first, out_ref):
    height, width = plane.shape
    columns = out_ref.shape[1]

    def one(v, carry):
        moved = pltpu.roll(plane, width - first - v, axis=1)[:, :columns]
        start = pl.multiple_of(v * height, height)
        out_ref[pl.ds(start, height), :] = moved.astype(bf16)
        return carry

    lax.fori_loop(0, taps, one, 0, unroll=UNROLL["stack"])
    rest = out_ref.shape[0] - taps * height
    out_ref[taps * height :, :] = jnp.zeros((rest, columns), bf16)


def forward_kernel(
    taps,
    reach,
    gain_ref,
    mask_ref,
    table_ref,
    pix_ref,
    count_ref,
    level_ref,
    table_hbm,
    stack_ref,
    lines_ref,
    sem,
):
    columns = stack_ref.shape[1]
    halves = columns // LANES
    rows = lines_ref.shape[0] // halves
    store = pltpu.make_async_copy(table_ref, table_hbm, sem.at[0])
    store.start()
    plane = mask_ref[reach : reach + rows + 2 * reach, :].astype(f32)
    stack_shifts(plane, taps, reach, stack_ref)
    fields = jnp.dot(table_ref[...], stack_ref[...], preferred_element_type=f32)
    total = jnp.zeros((rows, columns), f32)
    for k in range(gain_ref.shape[0]):
        real = fields[2 * k * rows : (2 * k + 1) * rows]
        imag = fields[(2 * k + 1) * rows : (2 * k + 2) * rows]
        total = total + gain_ref[k] * (real * real + imag * imag)
    for half in range(halves):
        lines_ref[half * rows : (half + 1) * rows, :] = total[:, half * LANES : (half + 1) * LANES]
    pix = pix_ref[...]
    slots, owners = pix.shape
    low = pix & (LANES - 1)
    high = pix >> 7

    def pick(i, level):
        for half in range(halves):
            line = lines_ref[pl.ds(half * rows + i, 1), :]
            wide = jnp.broadcast_to(line, (slots, LANES))
            found = jnp.take_along_axis(wide, low, axis=1, mode="promise_in_bounds")
            level = jnp.where(high == i * halves + half, found, level)
        return level

    level = lax.fori_loop(0, rows, pick, jnp.zeros((slots, owners), f32), unroll=UNROLL["pick"])
    live = lax.broadcasted_iota(jnp.int32, (slots, owners), 0) < count_ref[...]
    level = jnp.where(live, level, -1.0)
    level = jnp.concatenate([level, jnp.zeros((owners - slots, owners), f32)], axis=0)
    level_ref[...] = level.T
    store.wait()


def stack_wide_shifts(plane, taps, columns, extra, stack_ref):
    width = plane.shape[1]
    height = stack_ref.shape[0] // taps // 8 * 8
    lane = lax.broadcasted_iota(jnp.int32, (height, width - columns), 1)

    def one(v, carry):
        moved = pltpu.roll(plane, width - v, axis=1)
        first, second = moved[:height], moved[plane.shape[0] - height :]
        rest = pltpu.roll(second[:, columns:], extra, axis=1)
        rest = jnp.where(lane < extra, first[:, columns:], rest)
        start = pl.multiple_of(v * height, height)
        stack_ref[pl.ds(start, height), :columns] = first[:, :columns].astype(bf16)
        stack_ref[pl.ds(start, height), columns : 2 * columns] = second[:, :columns].astype(bf16)
        stack_ref[pl.ds(start, height), 2 * columns :] = rest.astype(bf16)
        return carry

    lax.fori_loop(0, taps, one, 0, unroll=UNROLL["wide"])
    rest = stack_ref.shape[0] - taps * height
    stack_ref[taps * height :, :] = jnp.zeros((rest, stack_ref.shape[1]), bf16)


def wide_kernel(
    taps,
    columns,
    extra,
    gain_ref,
    near_ref,
    table_hbm,
    fields_hbm,
    inten_ref,
    fields_ref,
    table_ref,
    stack_ref,
    in_sem,
    out_sems,
):
    load = pltpu.make_async_copy(table_hbm, table_ref, in_sem.at[0])
    load.start()
    stack_wide_shifts(near_ref[...].astype(f32), taps, columns, extra, stack_ref)
    load.wait()
    fields = jnp.dot(table_ref[...], stack_ref[...], preferred_element_type=f32)
    size = fields.shape[0]
    lanes = fields.shape[1] - 2 * columns
    rows = inten_ref.shape[0] // 2
    stores = []
    for half in range(2):
        ends = fields[:, 2 * columns :]
        if half:
            ends = pltpu.roll(ends, lanes - extra, axis=1)
        part = pl.ds(half * size, size)
        fields_ref[part, :columns] = fields[:, half * columns : (half + 1) * columns]
        fields_ref[part, columns:] = ends
        stores.append(
            pltpu.make_async_copy(fields_ref.at[part], fields_hbm.at[part], out_sems.at[half])
        )
        stores[-1].start()
    for half in range(2):
        total = jnp.zeros((rows, inten_ref.shape[1]), f32)
        for k in range(gain_ref.shape[0]):
            start = half * size + 2 * k * rows
            real = fields_ref[start : start + rows, :]
            imag = fields_ref[start + rows : start + 2 * rows, :]
            total = total + gain_ref[k] * (real * real + imag * imag)
        inten_ref[half * rows : (half + 1) * rows, :] = total
    for store in stores:
        store.wait()


def spread(value, index, size):
    here = lax.broadcasted_iota(jnp.int32, (size, LANES), 0) == index
    return jnp.where(here, value, 0.0).astype(bf16)


def product_nt(a, b):
    return lax.dot_general(a, b, (((1,), (1,)), ((), ())), preferred_element_type=f32)


def side_by_side(ref):
    return jnp.concatenate([ref[c] for c in range(ref.shape[0])], axis=1)


def owner_kernel(
    grid_rows,
    grid_cols,
    dose_ref,
    level_ref,
    frag_ref,
    aim_ref,
    error_ref,
    slope_ref,
    level_t,
    slope_t,
    resist_ref,
    value_ref,
    place_ref,
    around_t,
):
    slots = frag_ref.shape[0]
    conds = dose_ref.shape[0]
    bins = aim_ref.shape[1] // LANES
    level_t[...] = level_ref[...].T
    dose = jnp.broadcast_to(dose_ref[...], (conds, LANES))

    def place(c, carry):
        level = jnp.broadcast_to(level_t[pl.ds(c, 1), :], (conds, LANES))
        resist = jax.nn.sigmoid(steepness * (dose * level - threshold))
        live = level >= 0.0
        resist_ref[c] = jnp.where(live, resist, 0.0)
        frag = frag_ref[pl.ds(c, 1), :]
        bin_of = jnp.broadcast_to(frag >> 7, (conds, LANES))
        value_ref[c] = jnp.concatenate(
            [jnp.where(bin_of == q, resist_ref[c], 0.0) for q in range(bins)], axis=0
        ).astype(bf16)
        place_ref[c] = spread(1.0, frag & (LANES - 1), LANES)
        return carry

    lax.fori_loop(0, slots, place, 0, unroll=UNROLL["owner"])
    total = product_nt(side_by_side(value_ref), side_by_side(place_ref))
    for q in range(bins):
        lanes = slice(q * LANES, (q + 1) * LANES)
        error_ref[:, lanes] = total[q * conds : (q + 1) * conds] - aim_ref[:, lanes]

    def answer(c, carry):
        resist = resist_ref[c]
        frag = jnp.broadcast_to(frag_ref[pl.ds(c, 1), :], (conds, LANES))
        low = frag & (LANES - 1)
        bin_of = frag >> 7
        reply = jnp.zeros((conds, LANES), f32)
        for q in range(bins):
            found = jnp.take_along_axis(
                error_ref[:, q * LANES : (q + 1) * LANES], low, axis=1, mode="promise_in_bounds"
            )
            reply = jnp.where(bin_of == q, found, reply)
        terms = reply * steepness * dose * resist * (1.0 - resist)
        slope_t[pl.ds(c, 1), :] = jnp.sum(terms, axis=0, keepdims=True)
        return carry

    lax.fori_loop(0, slots, answer, 0, unroll=UNROLL["answer"])
    slope = slope_t[:slots, :]
    lane = lax.broadcasted_iota(jnp.int32, (slots, LANES), 1)
    tile_row, tile_col = lane // grid_cols, lane % grid_cols
    for t, (down, right) in enumerate(NEIGHBOURS):
        row, col = tile_row + down, tile_col + right
        inside = (row >= 0) & (row < grid_rows) & (col >= 0) & (col < grid_cols)
        moved = pltpu.roll(slope, -(down * grid_cols + right) % LANES, axis=1)
        around_t[t * slots : (t + 1) * slots, :] = jnp.where(inside, moved, 0.0)
    rest = around_t.shape[0] - len(NEIGHBOURS) * slots
    around_t[len(NEIGHBOURS) * slots :, :] = jnp.zeros((rest, LANES), f32)
    for block in range(around_t.shape[0] // LANES):
        slope_ref[:, block, :] = around_t[block * LANES : (block + 1) * LANES, :].T


def shift_right(x, by):
    assert by & (by - 1) == 0
    return x >> (by.bit_length() - 1)


def place_sites(
    tile_rows, columns, reach, slots, reply_t, pix_refs, first_ref, second_ref, value_ref, place_ref, tall_ref, flat_ref
):
    halves = columns // LANES
    for t, (down, right) in enumerate(NEIGHBOURS):
        pix = pix_refs[right + 1][(down + 1) * slots : (down + 2) * slots, :]
        row, col = shift_right(pix, columns), pix & (columns - 1)
        row = row - (tile_rows - reach) if down < 0 else row
        height = reach if down else tile_rows
        block = pl.ds(t * slots, slots)
        if right:
            first_ref[block, :] = row
            second_ref[block, :] = col - (columns - reach) if right < 0 else col
        else:
            inside = (row >= 0) & (row < height)
            line = shift_right(col, LANES) * height + row
            first_ref[block, :] = jnp.where(inside, line, -1)
            second_ref[block, :] = col & (LANES - 1)

    def one(c, carry):
        value, where, tall, flat = [], [], [], []
        narrow, narrow_where = [], []
        for t, (down, right) in enumerate(NEIGHBOURS):
            reply = reply_t[pl.ds(t * slots + c, 1), :]
            first = first_ref[pl.ds(t * slots + c, 1), :]
            second = second_ref[pl.ds(t * slots + c, 1), :]
            height = reach if down else tile_rows
            if right:
                narrow.append(spread(reply, first, height))
                narrow_where.append(spread(1.0, second, reach))
                continue
            part = spread(reply, first, halves * height)
            (tall if down else value).append(part)
            (flat if down else where).append(spread(1.0, second, LANES))
        value_ref[c] = jnp.concatenate(value + narrow, axis=0)
        rest = jnp.zeros((place_ref.shape[1] - LANES - len(narrow_where) * reach, LANES), bf16)
        place_ref[c] = jnp.concatenate(where + narrow_where + [rest], axis=0)
        tall_ref[c] = jnp.concatenate(tall, axis=0)
        flat_ref[c] = jnp.concatenate(flat, axis=0)
        return carry

    lax.fori_loop(0, slots, one, 0, unroll=UNROLL["site"])


def finish_kernel(
    taps,
    slots,
    grid_rows,
    grid_cols,
    gain_ref,
    reply_ref,
    low_ref,
    pix_ref,
    high_ref,
    target_ref,
    inten_ref,
    fields_hbm,
    table_hbm,
    out_ref,
    fields_ref,
    table_ref,
    reply_t,
    first_ref,
    second_ref,
    value_ref,
    place_ref,
    tall_ref,
    flat_ref,
    weighted_ref,
    part_ref,
    sems,
):
    fields_copy = pltpu.make_async_copy(fields_hbm, fields_ref, sems.at[0])
    table_copy = pltpu.make_async_copy(table_hbm, table_ref, sems.at[1])
    fields_copy.start()
    table_copy.start()
    rows, columns = out_ref.shape
    height, width = inten_ref.shape
    reach = (height - rows) // 2
    halves = columns // LANES
    for block in range(reply_ref.shape[1]):
        reply_t[block * LANES : (block + 1) * LANES, :] = reply_ref[:, block, :].T
    pix_refs = (low_ref, pix_ref, high_ref)
    place_sites(
        rows, columns, reach, slots, reply_t, pix_refs, first_ref, second_ref, value_ref, place_ref, tall_ref, flat_ref
    )
    near_sum = product_nt(side_by_side(value_ref), side_by_side(place_ref))
    tall_sum = product_nt(side_by_side(tall_ref), side_by_side(flat_ref))

    def across(block, size):
        return jnp.concatenate(
            [block[half * size : (half + 1) * size] for half in range(halves)]
            + [jnp.zeros((size, width - columns), f32)],
            axis=1,
        )

    middle = near_sum[: halves * rows, :LANES]
    above = tall_sum[: halves * reach, :LANES]
    below = tall_sum[halves * reach :, LANES : 2 * LANES]
    scattered = jnp.concatenate(
        [across(above, reach), across(middle, rows), across(below, reach)], axis=0
    )
    scattered = pltpu.roll(scattered, reach, axis=1)
    start = halves * rows
    lane = lax.broadcasted_iota(jnp.int32, (height, LANES), 1)
    sides = []
    for side in range(2):
        strips = []
        for place in range(3):
            size = rows if place == 1 else reach
            strip = near_sum[start : start + size, LANES : 2 * LANES]
            shift = (side * reach - (side * 3 + place) * reach) % LANES
            strips.append(pltpu.roll(strip, shift, axis=1) if shift else strip)
            start += size
        strip = jnp.concatenate(strips, axis=0)
        here = (lane >= side * reach) & (lane < (side + 1) * reach)
        sides.append(jnp.where(here, strip, 0.0))
    gap = jnp.zeros((height, LANES), f32)
    strips = [sides[0]] + [gap] * (halves - 1) + [sides[1]]

    nominal = jax.nn.sigmoid(steepness * (inten_ref[...] - threshold))
    first = pix_ref.shape[0]
    target = jnp.concatenate([low_ref[first:, :], target_ref[...], high_ref[first:, :]], axis=1)
    target = pltpu.roll(target.astype(f32), target.shape[1] - (LANES - reach), axis=1)
    dense = (nominal - target[:, :width]) * steepness * nominal * (1.0 - nominal)
    slope = dense + scattered + jnp.concatenate(strips, axis=1)
    line = lax.broadcasted_iota(jnp.int32, (height, width), 0) - reach
    line = line + lax.axis_index("row") * rows
    column = lax.broadcasted_iota(jnp.int32, (height, width), 1) - reach
    inside = (column < columns + reach) & (line >= 0) & (line < grid_rows * rows)
    column = column + lax.axis_index("col") * columns
    inside = inside & (column >= 0) & (column < grid_cols * columns)
    slope = jnp.where(inside, slope, 0.0)

    upper = height // 2
    parts = weighted_ref.shape[0] // height

    def weigh(h, carry):
        for half in range(2):
            lines = pl.ds(pl.multiple_of((half * parts + h) * upper, upper), upper)
            weight = gain_ref[h // 2] * fields_ref[lines, :]
            lines = pl.ds(pl.multiple_of(h * height + half * upper, upper), upper)
            weighted = weight * slope[half * upper : (half + 1) * upper]
            weighted_ref[lines, :] = weighted.astype(bf16)
        return carry

    fields_copy.wait()
    lax.fori_loop(0, weighted_ref.shape[0] // height, weigh, 0, unroll=UNROLL["weigh"])
    table_copy.wait()
    part_ref[...] = jnp.dot(table_ref[...], weighted_ref[...], preferred_element_type=f32)

    def gather(v, total):
        start = pl.multiple_of(v * rows, rows)
        return total + pltpu.roll(part_ref[pl.ds(start, rows), :], width - v, axis=1)[:, :columns]

    total = jnp.zeros((rows, columns), f32)
    total = lax.fori_loop(0, taps, gather, total, unroll=UNROLL["gather"])
    out_ref[...] = 2.0 * total


def round_up(x, to):
    return -(-x // to) * to


def lines_of(taps, stride, length):
    count, blocks, extent = taps.shape
    padded = jnp.pad(taps, ((0, 0), (0, 0), (0, stride - extent)))
    flat = padded.reshape(count, blocks * stride)
    return jnp.pad(flat, ((0, 0), (0, length - blocks * stride))).astype(f32)


def body(mask, target, kernels, weights, doses, site_pix, send_count, recv_frag, frag_target):
    rows, columns = mask.shape
    extent = kernels.shape[-1]
    reach = extent // 2
    kernel_taps = kernels.reshape(-1, extent, extent)
    parts = kernel_taps.shape[0]
    owners, slots = site_pix.shape
    conds = doses.shape[0]
    both = ("row", "col")

    wide = 2 * reach
    pix = site_pix.T
    low, high = clipped(*ring(mask[:wide], mask[rows - wide :], "row"), "row")
    near = jnp.concatenate([low, mask, high], axis=0)
    near, pix, target = lax.optimization_barrier((near, pix, target))
    low, high = clipped(*ring(near[:, :wide], near[:, columns - wide :], "col"), "col")
    near = jnp.concatenate([low, near, high], axis=1)
    wide_columns = round_up(near.shape[1], LANES)
    near = jnp.pad(near, ((0, 0), (0, wide_columns - near.shape[1])))

    halves = columns // LANES

    def pixels_and(aim):
        lanes = [aim[:, half * LANES : (half + 1) * LANES] for half in range(halves)]
        return jnp.concatenate([pix] + lanes, axis=0)

    low, high = ring(pixels_and(target[:reach]), pixels_and(target[rows - reach :]), "row")
    pix_column = jnp.concatenate([low[:slots], pix, high[:slots]], axis=0)
    target_column = jnp.concatenate(
        [
            jnp.concatenate(
                [side[slots + half * reach :][:reach] for half in range(halves)], axis=1
            )
            if side is not None
            else target
            for side in (low, None, high)
        ],
        axis=0,
    )

    height = rows + 2 * reach
    by_column = kernel_taps.transpose(0, 2, 1)
    core_depth = round_up(extent * height, LANES)
    core_shape = (parts * rows, core_depth)
    core_table = call(
        functools.partial(table_kernel, rows),
        jax.ShapeDtypeStruct(core_shape, bf16),
        inputs=1,
        moved=2 * parts * rows * core_depth,
    )(lines_of(by_column, height, core_depth))

    level, stored_table = call(
        functools.partial(forward_kernel, extent, reach),
        (jax.ShapeDtypeStruct((owners, LANES), f32), pltpu.HBM(core_shape, bf16)),
        scratch=[
            pltpu.VMEM((core_depth, columns), bf16),
            pltpu.VMEM((rows * columns // LANES, LANES), f32),
            pltpu.SemaphoreType.DMA((1,)),
        ],
        inputs=5,
        smem=(0,),
        hbm_out=(1,),
        flops=2 * parts * rows * core_depth * columns,
        moved=2 * parts * rows * core_depth,
    )(weights, near, core_table, pix, send_count)

    flipped = kernel_taps[:, ::-1, ::-1].transpose(2, 0, 1)
    back_depth = parts * height
    level, pix_column, target_column, back_lines = lax.optimization_barrier(
        (level, pix_column, target_column, lines_of(flipped, height, back_depth))
    )
    arrived = lax.all_to_all(level, both, split_axis=0, concat_axis=0, tiled=True)
    back_shape = (extent * rows, back_depth)
    (back_table,) = call(
        functools.partial(back_table_kernel, rows),
        (pltpu.HBM(back_shape, bf16),),
        scratch=[pltpu.VMEM(back_shape, bf16), pltpu.SemaphoreType.DMA((1,))],
        inputs=1,
        hbm_out=(0,),
        moved=2 * extent * rows * back_depth,
    )(back_lines)
    arrived, back_table = lax.optimization_barrier((arrived, back_table))
    low, high = ring(
        jnp.concatenate([pix_column, target_column[:, :LANES]], axis=0),
        jnp.concatenate([pix_column, target_column[:, columns - LANES :]], axis=0),
        "col",
    )
    grid_rows, grid_cols = lax.axis_size("row"), lax.axis_size("col")
    blocks = round_up(len(NEIGHBOURS) * slots, LANES) // LANES
    frag_error, answers = call(
        functools.partial(owner_kernel, grid_rows, grid_cols),
        (
            jax.ShapeDtypeStruct(frag_target.shape, f32),
            jax.ShapeDtypeStruct((owners, blocks, LANES), f32),
        ),
        scratch=[
            pltpu.VMEM((LANES, LANES), f32),
            pltpu.VMEM((slots, LANES), f32),
            pltpu.VMEM((slots, conds, LANES), f32),
            pltpu.VMEM((slots, frag_target.size // LANES, LANES), bf16),
            pltpu.VMEM((slots, LANES, LANES), bf16),
            pltpu.VMEM((blocks * LANES, LANES), f32),
        ],
        inputs=4,
        flops=2 * 2 * frag_target.size * site_pix.size // 16,
        moved=8 * frag_target.size,
    )(doses[:, None], arrived, recv_frag.T, frag_target)

    answers, near = lax.optimization_barrier((answers, near))
    returned = lax.all_to_all(answers, both, split_axis=0, concat_axis=0, tiled=True)
    wide_fields, wide_intensity = call(
        functools.partial(wide_kernel, extent, columns, wide),
        (
            pltpu.HBM((parts * height, wide_columns), f32),
            jax.ShapeDtypeStruct((height, wide_columns), f32),
        ),
        scratch=[
            pltpu.VMEM((parts * height, wide_columns), f32),
            pltpu.VMEM(core_shape, bf16),
            pltpu.VMEM((core_depth, columns + wide_columns), bf16),
            pltpu.SemaphoreType.DMA((1,)),
            pltpu.SemaphoreType.DMA((2,)),
        ],
        inputs=3,
        smem=(0,),
        hbm=(2,),
        hbm_out=(0,),
        vmem_mib=24,
        flops=2 * parts * rows * core_depth * (columns + wide_columns),
        moved=4 * parts * height * wide_columns,
    )(weights, near, pltpu.with_memory_space_constraint(stored_table, pltpu.HBM))
    returned, wide_fields, wide_intensity, low, high = lax.optimization_barrier(
        (returned, wide_fields, wide_intensity, low, high)
    )
    wide_fields = pltpu.with_memory_space_constraint(wide_fields, pltpu.HBM)
    back_table = pltpu.with_memory_space_constraint(back_table, pltpu.HBM)
    gradient = call(
        functools.partial(finish_kernel, extent, slots, grid_rows, grid_cols),
        jax.ShapeDtypeStruct((rows, columns), f32),
        scratch=[
            pltpu.VMEM(wide_fields.shape, f32),
            pltpu.VMEM(back_table.shape, bf16),
            pltpu.VMEM((blocks * LANES, LANES), f32),
            pltpu.VMEM((blocks * LANES, LANES), jnp.int32),
            pltpu.VMEM((blocks * LANES, LANES), jnp.int32),
            pltpu.VMEM((slots, halves * rows + 2 * (rows + 2 * reach), LANES), bf16),
            pltpu.VMEM((slots, 2 * LANES, LANES), bf16),
            pltpu.VMEM((slots, 2 * halves * reach, LANES), bf16),
            pltpu.VMEM((slots, 2 * LANES, LANES), bf16),
            pltpu.VMEM((back_depth, wide_columns), bf16),
            pltpu.VMEM((extent * rows, wide_columns), f32),
            pltpu.SemaphoreType.DMA((2,)),
        ],
        inputs=9,
        smem=(0,),
        hbm=(7, 8),
        vmem_mib=32,
        flops=2 * extent * rows * back_depth * wide_columns,
        moved=8 * back_depth * wide_columns,
    )(
        weights,
        returned,
        low,
        pix_column,
        high,
        target_column,
        wide_intensity,
        wide_fields,
        back_table,
    )
    return gradient, frag_error


def solution(mesh):
    return jax.shard_map(
        body,
        mesh=mesh,
        in_specs=(
            P("row", "col"),
            P("row", "col"),
            P(),
            P(),
            P(),
            P("row", "col"),
            P("row", "col"),
            P("row", "col"),
            P(None, ("row", "col")),
        ),
        out_specs=(P("row", "col"), P(None, ("row", "col"))),
        check_vma=False,
    )
```
